256 devices in a mesh: ctx: 16 (over z, core), head: 4 (over y), rep: 4 (over x).
Axes of the slice: x: 4, y: 4, z: 8, core: 2. Of those that a mesh axis runs over, the one named last changes fastest.
Arguments:
- kv_cache: float32 [8, 2, 4096, 8, 128], P('head', None, 'ctx', 'rep'), may hold values from -8 to 8
- prefill_q: float32 [8, 256, 64, 128], P('head', 'ctx', 'rep'), may hold values from -512 to 512
- decode_q: float32 [8, 64, 4, 64, 128], P(None, ('ctx', 'rep'), None, 'head'), may hold values from -512 to 512
- decode_kv: float32 [8, 64, 4, 2, 8, 128], P(None, ('ctx', 'rep'), None, None, 'head'), may hold values from -12 to 12
- lengths: int32 [8], replicated, may hold values from 1024 to 4096, as said below
- row_length: int32 [8, 64], P(None, ('ctx', 'rep')), may hold values from 2 to 4096, as said below
Outputs:
- prefill_out: float32 [8, 256, 64, 128], P('head', 'ctx', 'rep')
- decode_out: float32 [8, 64, 4, 64, 128], P(None, ('ctx', 'rep'), None, 'head')
The draws below stay inside these ranges and needn't reach their ends.
Inputs may be any that keep to these rules, and one draw needn't show every extreme that they name: `lengths`: multiples of 128; some request has length 4096. `row_length`: a row reads at most its request's length; every request has a row that reads its whole length.
All inputs are finite; a program needn't handle non-finite values.
Results may differ from the reference program's by a relative error of at most 0.0003.
Values sent between devices are 32-bit elements; how exact they have to be, the bound alone decides.
A program may use at most 128 MiB of HBM per device.

```python
import math
import jax
import jax.numpy as jnp
from jax import lax

HD = 128
KVH = 8
QH = 64
REQS = 8
LMAX = 4096
GRAIN = 128
SPAN = 256
STEPS = 4
ROWS_REQ = 64


def length_table(key):
    base_key = jax.random.fold_in(key, 7)
    lowest = max(SPAN, LMAX // 4 // GRAIN * GRAIN) // GRAIN
    unit_counts = jax.random.randint(jax.random.fold_in(base_key, 1), (REQS,), lowest, LMAX // GRAIN + 1)
    longest = jax.random.randint(jax.random.fold_in(base_key, 2), (), 0, REQS)
    unit_counts = jnp.where(jnp.arange(REQS) == longest, LMAX // GRAIN, unit_counts)
    return (unit_counts * GRAIN).astype(jnp.int32)


def draw_lengths(key, part):
    return length_table(key)


def draw_row_length(key, part):
    totals = length_table(key)
    base_key = jax.random.fold_in(key, 8)
    raw_bits = jax.random.randint(jax.random.fold_in(base_key, 1), (REQS, ROWS_REQ), 0, 1 << 30)
    drawn = 2 + raw_bits % (totals[:, None] - 1)
    full_row = jax.random.randint(jax.random.fold_in(base_key, 2), (REQS,), 0, ROWS_REQ)
    drawn = jnp.where(jnp.arange(ROWS_REQ)[None, :] == full_row[:, None], totals[:, None], drawn)
    return drawn.astype(jnp.int32)


def draw_kv_cache(key, part):
    own_key = jax.random.fold_in(key, 21)
    drawn_shape = (REQS, 2, LMAX, KVH, HD)
    drawn = jnp.clip(jax.random.normal(own_key, drawn_shape), -6.0, 6.0)
    return drawn.astype(jnp.float32)


def draw_prefill_q(key, part):
    own_key = jax.random.fold_in(key, 31)
    drawn_shape = (REQS, SPAN, QH, HD)
    drawn = 2.5 * jnp.clip(jax.random.normal(own_key, drawn_shape), -6.0, 6.0)
    return jnp.clip(drawn, -500.0, 500.0).astype(jnp.float32)


def draw_decode_q(key, part):
    own_key = jax.random.fold_in(key, 41)
    drawn_shape = (REQS, ROWS_REQ, STEPS, QH, HD)
    drawn = 2.5 * jnp.clip(jax.random.normal(own_key, drawn_shape), -6.0, 6.0)
    return jnp.clip(drawn, -500.0, 500.0).astype(jnp.float32)


def block_levels(key, shape, split, smallest, largest):
    def one(axis_at, shards_of):
        draws = jax.random.uniform(jax.random.fold_in(jax.random.fold_in(key, 6), axis_at), (shards_of,), jnp.float32, smallest / len(split), largest / len(split))
        return jnp.repeat(jnp.exp(draws), shape[axis_at] // shards_of).reshape((-1,) + (1,) * (len(shape) - axis_at - 1))

    loudness = one(*split[0])
    for cut in split[1:]:
        loudness = loudness * one(*cut)
    return loudness


def normal_values(stream_key, extent, deviation, most, cuts=(), kind=jnp.bfloat16):
    entries = deviation * jax.random.normal(stream_key, extent, jnp.float32)
    if cuts:
        entries = entries * block_levels(stream_key, extent, cuts, -0.22, 0.18)
    return jnp.clip(entries, -most, most).astype(kind)


def setup_inputs(seed: int = 0) -> dict:
    splits = jax.random.split(jax.random.key(seed), 7)
    kv_cache = draw_kv_cache(jax.random.fold_in(splits[6], 71), 0)
    prefill_q = draw_prefill_q(jax.random.fold_in(splits[6], 71), 0)
    decode_q = draw_decode_q(jax.random.fold_in(splits[6], 71), 0)
    decode_kv = normal_values(splits[3], (REQS, ROWS_REQ, STEPS, 2, KVH, HD), 2.0, 12.0, ((1, 64), (4, 4)), jnp.float32)
    lengths = draw_lengths(jax.random.fold_in(splits[6], 71), 0)
    row_length = draw_row_length(jax.random.fold_in(splits[6], 71), 0)
    return {"kv_cache": kv_cache, "prefill_q": prefill_q, "decode_q": decode_q, "decode_kv": decode_kv, "lengths": lengths, "row_length": row_length}


NEG_FILL = -1e+30
HIGH_PRECISION = lax.Precision.HIGHEST

def prefill_one(inputs):
    queries, cache_rows, length = inputs
    score_scale = 1.0 / math.sqrt(HD)
    grouped = queries.reshape(SPAN, KVH, QH // KVH, HD)
    scores = jnp.einsum('qkgd,pkd->kgqp', grouped, cache_rows[0], precision=HIGH_PRECISION) * score_scale
    query_pos = length - SPAN + jnp.arange(SPAN, dtype=jnp.int32)
    allowed = jnp.arange(LMAX, dtype=jnp.int32)[None, :] <= query_pos[:, None]
    scores = jnp.where(allowed[None, None], scores, NEG_FILL)
    weights = jax.nn.softmax(scores, axis=-1)
    blended = jnp.einsum('kgqp,pkd->qkgd', weights, cache_rows[1], precision=HIGH_PRECISION)
    return blended.reshape(SPAN, QH, HD)

def decode_one(inputs):
    queries, drafts, cache_rows, limits = inputs
    score_scale = 1.0 / math.sqrt(HD)
    grouped = queries.reshape(ROWS_REQ, STEPS, KVH, QH // KVH, HD)
    context = jnp.einsum('rtkgd,pkd->rtkgp', grouped, cache_rows[0], precision=HIGH_PRECISION) * score_scale
    visible = jnp.arange(LMAX, dtype=jnp.int32)[None, :] < limits[:, None]
    context = jnp.where(visible[:, None, None, None, :], context, NEG_FILL)
    own_scores = jnp.einsum('rtkgd,rskd->rtkgs', grouped, drafts[:, :, 0], precision=HIGH_PRECISION) * score_scale
    step_ids = jnp.arange(STEPS, dtype=jnp.int32)
    causal = step_ids[None, :] <= step_ids[:, None]
    own_scores = jnp.where(causal[None, :, None, None, :], own_scores, NEG_FILL)
    weights = jax.nn.softmax(jnp.concatenate([context, own_scores], axis=-1), axis=-1)
    blended = jnp.einsum('rtkgp,pkd->rtkgd', weights[..., :LMAX], cache_rows[1], precision=HIGH_PRECISION)
    blended = blended + jnp.einsum('rtkgs,rskd->rtkgd', weights[..., LMAX:], drafts[:, :, 1], precision=HIGH_PRECISION)
    return blended.reshape(ROWS_REQ, STEPS, QH, HD)

def reference(kv_cache, prefill_q, decode_q, decode_kv, lengths, row_length):
    prefill_out = lax.map(prefill_one, (prefill_q, kv_cache, lengths))
    decode_out = lax.map(decode_one, (decode_q, decode_kv, kv_cache, row_length))
    return (prefill_out, decode_out)
```

```python
import functools
import math

import jax
import jax.numpy as jnp
from jax import lax
from jax.experimental import pallas as pl
from jax.experimental.pallas import tpu as pltpu
from jax.sharding import PartitionSpec as P

MESH = pl.DeviceIdType.MESH
NEG_FILL = -1e30
F32 = jnp.float32
BF16 = jnp.bfloat16
CHIPS = 8
NQ = 1024
HALF = 512
BLK = 256
QC = 256


def split2(x):
    hi = x.astype(BF16)
    return hi, (x - hi.astype(F32)).astype(BF16)


def split3(x):
    hi = x.astype(BF16)
    rest = x - hi.astype(F32)
    mid = rest.astype(BF16)
    return hi, mid, (rest - mid.astype(F32)).astype(BF16)


def key_terms(k):
    hi, mid, lo = split3(k)
    return jnp.concatenate([hi, hi, mid, mid, hi, lo], axis=1)


def query_terms(q):
    hi, mid, lo = split3(q)
    return jnp.concatenate([hi, mid, hi, mid, lo, hi], axis=1)


def value_terms(v):
    hi, lo = split2(v.T)
    return jnp.concatenate([hi, lo], axis=0)


def dot_nt(a, b):
    return lax.dot_general(a, b, (((1,), (1,)), ((), ())), preferred_element_type=F32)


def weighted(v2, p):
    hi, lo = split2(p)
    both = jnp.dot(v2, hi, preferred_element_type=F32) + jnp.dot(v2, lo, preferred_element_type=F32)
    return both[:128] + both[128:]


def kernel(
    scale,
    span,
    len_ref,
    rl_ref,
    kv_ref,
    pq_ref,
    dq_ref,
    dkv_ref,
    po_ref,
    do_ref,
    raw,
    sendb,
    kvb,
    qb,
    lb,
    db,
    q6,
    k6,
    v2b,
    lim,
    m_ref,
    l_ref,
    acc,
    ob,
    sem_local,
    sem_pq_s,
    sem_pq_r,
    sem_dq_s,
    sem_dq_r,
    sem_kp_s,
    sem_kf_s,
    sem_kx_s,
    sem_k_r,
    sem_po_s,
    sem_po_r,
    sem_do_s,
    sem_do_r,
):
    c = lax.axis_index("ctx")
    y = lax.axis_index("head")
    x = lax.axis_index("rep")
    z = c // 2
    core = c % 2

    def dest(t):
        even = (z + t) % 2 == 0
        return lax.rem(jnp.where(even, z + t, z - t + CHIPS), CHIPS)

    def source_of(chip, t):
        return lax.rem(jnp.where(chip % 2 == 0, chip - t + CHIPS, chip + t), CHIPS)

    mate = z + 1 - 2 * (z % 2)
    pair = z // 2
    own_i = pair // 2
    own_j = pair % 2
    diag = x == y

    load = pltpu.make_async_copy(kv_ref, raw, sem_local.at[0])
    load.start()

    barrier = pltpu.get_barrier_semaphore()

    def greet(ctx, head, rep):
        pl.semaphore_signal(barrier, inc=1, device_id=(ctx, head, rep), device_id_type=MESH)

    greet(2 * z + 1 - core, y, x)
    greet(2 * mate + core, y, x)
    count = 2
    for t in range(4):
        to_c = 2 * dest(t) + core
        from_c = 2 * source_of(z, t) + core
        if t:
            greet(to_c, y, x)
            greet(from_c, y, x)
            count += 2
        for g in range(4):
            if t:
                greet(to_c, g, y)
                greet(from_c, x, g)
            else:

                @pl.when(jnp.logical_not((y == g) & diag))
                def _():
                    greet(to_c, g, y)
                    greet(from_c, x, g)

            count += 2

    load.wait()
    for i in range(2):
        for s in range(2):
            for j in range(2):
                sendb[2 * i + j, s] = raw[i, s, pl.ds(j, BLK, stride=2), :]

    pl.semaphore_wait(barrier, jnp.where(diag, count - 2, count))

    def pq_copy(t):
        zt = dest(t)
        p = zt // 2
        src = pq_ref.at[p // 2, :, pl.ds(pl.multiple_of(8 * (p % 2), 8), 8), :]
        dst = qb.at[pl.ds(16 * t, 16)]
        if t == 0:
            return pltpu.make_async_copy(src, dst, sem_pq_r.at[0])
        return pltpu.make_async_remote_copy(
            src, dst, sem_pq_s.at[t], sem_pq_r.at[t], device_id=(2 * zt + core, y, x), device_id_type=MESH
        )

    def dq_parts(t, g):
        p = dest(t) // 2
        req = 2 * g + p // 2
        slot = 4 * t + x
        return (
            (dq_ref.at[req, :, pl.ds(pl.multiple_of(8 * (p % 2), 8), 8), :], qb.at[pl.ds(64 + 4 * slot, 4)]),
            (dkv_ref.at[req], db.at[slot]),
            (rl_ref.at[req], lb.at[slot]),
        )

    def dq_remote(t, g, n, part):
        return pltpu.make_async_remote_copy(
            part[0],
            part[1],
            sem_dq_s.at[4 * t + g, n],
            sem_dq_r.at[4 * t + x, n],
            device_id=(2 * dest(t) + core, g, y),
            device_id_type=MESH,
        )

    def dq_start(t, g):
        for n, part in enumerate(dq_parts(t, g)):
            if t:
                dq_remote(t, g, n, part).start()
            else:
                mine = (y == g) & diag

                @pl.when(mine)
                def _():
                    pltpu.make_async_copy(part[0], part[1], sem_dq_r.at[4 * t + x, n]).start()

                @pl.when(jnp.logical_not(mine))
                def _():
                    dq_remote(t, g, n, part).start()

    def dq_wait_send(t, g):
        for n, part in enumerate(dq_parts(t, g)):
            if t:
                dq_remote(t, g, n, part).wait_send()
            else:

                @pl.when(jnp.logical_not((y == g) & diag))
                def _():
                    dq_remote(t, g, n, part).wait_send()

    def kv_primary(t):
        zt = dest(t)
        return pltpu.make_async_remote_copy(
            sendb.at[zt // 2],
            kvb.at[t],
            sem_kp_s.at[t],
            sem_k_r.at[t],
            device_id=(2 * zt + core, y, x),
            device_id_type=MESH,
        )

    def kv_forward(t):
        return pltpu.make_async_remote_copy(
            kvb.at[t],
            kvb.at[t + 4],
            sem_kf_s.at[t],
            sem_k_r.at[t + 4],
            device_id=(2 * mate + core, y, x),
            device_id_type=MESH,
        )

    def kv_cross(u):
        return pltpu.make_async_remote_copy(
            kvb.at[u],
            kvb.at[u + 8],
            sem_kx_s.at[u],
            sem_k_r.at[u + 8],
            device_id=(2 * z + 1 - core, y, x),
            device_id_type=MESH,
        )

    keep = pltpu.make_async_copy(sendb.at[pair], kvb.at[0], sem_k_r.at[0])
    keep.start()
    for t in (3, 2, 1, 0):
        pq_copy(t).start()
        for g in range(4):
            dq_start(t, g)
    for t in (3, 2, 1):
        kv_primary(t).start()

    def arrive(u):
        pltpu.make_async_copy(kvb.at[u], kvb.at[u], sem_k_r.at[u]).wait()

        @pl.when(u < 4)
        def _():
            kv_forward(u).start()

        @pl.when(u < 8)
        def _():
            kv_cross(u).start()

    arrive(jnp.int32(0))

    own_len = len_ref[2 * y + own_i]
    lane = lax.broadcasted_iota(jnp.int32, (1, 128), 1)
    for t in range(4):
        first = own_len - (span - 1) + 16 * (2 * source_of(z, t) + core)
        lim[:, pl.ds(128 * t, 128)] = first + lane // 8

    for t in range(4):
        part = qb.at[pl.ds(16 * t, 16)]
        pltpu.make_async_copy(part, part, sem_pq_r.at[t]).wait()

    @pl.loop(0, 16)
    def _(s):
        part = qb.at[pl.ds(64 + 4 * s, 4)]
        pltpu.make_async_copy(part, part, sem_dq_r.at[s, 0]).wait()
        pltpu.make_async_copy(db.at[s], db.at[s], sem_dq_r.at[s, 1]).wait()
        pltpu.make_async_copy(lb.at[s], lb.at[s], sem_dq_r.at[s, 2]).wait()

    for v in range(4):
        row = jnp.where(
            lane < 64,
            jnp.where(lane < 32, lb[4 * v], lb[4 * v + 1]),
            jnp.where(lane < 96, lb[4 * v + 2], lb[4 * v + 3]),
        )
        lim[:, pl.ds(HALF + 128 * v, 128)] = row

    @pl.loop(0, NQ // 128)
    def _(n):
        q = qb[pl.ds(16 * n, 16)].reshape(128, 128) * scale
        q6[pl.ds(pl.multiple_of(128 * n, 128), 128), :] = query_terms(q)

    m_ref[:, :HALF] = jnp.full((1, HALF), NEG_FILL, F32)
    l_ref[:, :HALF] = jnp.zeros((1, HALF), F32)
    acc[:, :HALF] = jnp.zeros((128, HALF), F32)
    drafts = db[...].reshape(64, 4, 128)
    dk = jnp.where(own_j == 0, drafts[:, 0], drafts[:, 1])
    dv = jnp.where(own_j == 0, drafts[:, 2], drafts[:, 3])
    s = dot_nt(key_terms(dk), q6[pl.ds(HALF, HALF), :])
    key_id = lax.broadcasted_iota(jnp.int32, (64, HALF), 0)
    query_id = lax.broadcasted_iota(jnp.int32, (64, HALF), 1) // 8
    s = jnp.where((key_id // 4 == query_id // 4) & (key_id <= query_id), s, NEG_FILL)
    top = jnp.max(s, axis=0, keepdims=True)
    p = jnp.exp2(s - top)
    m_ref[:, HALF:] = top
    l_ref[:, HALF:] = jnp.sum(p, axis=0, keepdims=True)
    acc[:, HALF:] = weighted(value_terms(dv), p)

    def order(n):
        return n // 4 + (n % 2) * 8 + ((n // 2) % 2) * 4

    @pl.loop(0, 16)
    def _(n):
        u = order(n)

        @pl.when(n < 15)
        def _():
            arrive(order(n + 1))

        t = u % 4
        chip = jnp.where((u // 4) % 2 == 0, z, mate)
        owner = jnp.where(u < 8, core, 1 - core)
        first = BLK * (2 * source_of(chip, t) + owner)
        k6[...] = key_terms(kvb[u, 0])
        v2b[...] = value_terms(kvb[u, 1])
        for qc in range(NQ // QC):
            cols = pl.ds(QC * qc, QC)
            s = dot_nt(k6[...], q6[pl.ds(QC * qc, QC), :])
            place = lax.broadcasted_iota(jnp.int32, (BLK, QC), 0)
            s = jnp.where(place < lim[:, cols] - first, s, NEG_FILL)
            old = m_ref[:, cols]
            top = jnp.maximum(old, jnp.max(s, axis=0, keepdims=True))
            fade = jnp.exp2(old - top)
            p = jnp.exp2(s - top)
            m_ref[:, cols] = top
            l_ref[:, cols] = l_ref[:, cols] * fade + jnp.sum(p, axis=0, keepdims=True)
            acc[:, cols] = acc[:, cols] * fade + weighted(v2b[...], p)

    rows_j = pl.ds(pl.multiple_of(8 * own_j, 8), 8)

    def po_copy(t):
        src = ob.at[pl.ds(16 * t, 16)]
        dst = po_ref.at[own_i, :, rows_j, :]
        if t == 0:
            return pltpu.make_async_copy(src, dst, sem_po_r.at[0])
        return pltpu.make_async_remote_copy(
            src,
            dst,
            sem_po_s.at[t],
            sem_po_r.at[t],
            device_id=(2 * source_of(z, t) + core, y, x),
            device_id_type=MESH,
        )

    def do_ends(t, r):
        return ob.at[pl.ds(64 + 16 * t + 4 * r, 4)], do_ref.at[2 * y + own_i, :, rows_j, :]

    def do_remote(t, r):
        src, dst = do_ends(t, r)
        return pltpu.make_async_remote_copy(
            src,
            dst,
            sem_do_s.at[4 * t + r],
            sem_do_r.at[4 * t + y],
            device_id=(2 * source_of(z, t) + core, x, r),
            device_id_type=MESH,
        )

    def do_start(t, r):
        if t:
            do_remote(t, r).start()
            return
        mine = (x == r) & diag

        @pl.when(mine)
        def _():
            src, dst = do_ends(t, r)
            pltpu.make_async_copy(src, dst, sem_do_r.at[4 * t + y]).start()

        @pl.when(jnp.logical_not(mine))
        def _():
            do_remote(t, r).start()

    for qc in (3, 1, 2, 0):
        cols = pl.ds(QC * qc, QC)
        out = acc[:, cols] * (1.0 / l_ref[:, cols])
        ob[pl.ds(32 * qc, 32)] = out.T.reshape(32, 8, 128)
        for t in (2 * (qc % 2) + 1, 2 * (qc % 2)):
            if qc < 2:
                po_copy(t).start()
            else:
                for r in range(4):
                    do_start(t, r)

    for t in range(1, 4):
        pq_copy(t).wait_send()
        kv_primary(t).wait_send()
    for t in range(4):
        for g in range(4):
            dq_wait_send(t, g)
        kv_forward(t).wait_send()
    for u in range(8):
        kv_cross(u).wait_send()
    for t in range(4):
        if t:
            po_copy(t).wait_send()
        p = dest(t) // 2
        rows = pl.ds(pl.multiple_of(8 * (p % 2), 8), 8)
        got = po_ref.at[p // 2, :, rows, :]
        pltpu.make_async_copy(got, got, sem_po_r.at[t]).wait()
        for g in range(4):
            if t:
                do_remote(t, g).wait_send()
            else:

                @pl.when(jnp.logical_not((x == g) & diag))
                def _():
                    do_remote(t, g).wait_send()

            got = do_ref.at[2 * g + p // 2, :, rows, :]
            pltpu.make_async_copy(got, got, sem_do_r.at[4 * t + g]).wait()


def on_device(kv_cache, prefill_q, decode_q, decode_kv, lengths, row_length):
    head_dim = prefill_q.shape[-1]
    span = prefill_q.shape[1] * lax.axis_size("ctx")
    scale = math.log2(math.e) / math.sqrt(head_dim)
    limits = jnp.broadcast_to(row_length[:, :, None], (8, 1, 128))
    hbm = pl.BlockSpec(memory_space=pltpu.MemorySpace.HBM)
    dma = pltpu.SemaphoreType.DMA
    prefill_out, decode_out = pl.pallas_call(
        functools.partial(kernel, scale, span),
        out_shape=(
            jax.ShapeDtypeStruct((2, 16, 16, 128), F32),
            jax.ShapeDtypeStruct((8, 4, 16, 128), F32),
        ),
        in_specs=[pl.BlockSpec(memory_space=pltpu.SMEM)] + [hbm] * 5,
        out_specs=(hbm, hbm),
        scratch_shapes=[
            pltpu.VMEM((2, 2, 512, 128), F32),
            pltpu.VMEM((4, 2, BLK, 128), F32),
            pltpu.VMEM((16, 2, BLK, 128), F32),
            pltpu.VMEM((128, 8, 128), F32),
            pltpu.VMEM((16, 1, 128), jnp.int32),
            pltpu.VMEM((16, 16, 128), F32),
            pltpu.VMEM((NQ, 768), BF16),
            pltpu.VMEM((BLK, 768), BF16),
            pltpu.VMEM((256, BLK), BF16),
            pltpu.VMEM((1, NQ), jnp.int32),
            pltpu.VMEM((1, NQ), F32),
            pltpu.VMEM((1, NQ), F32),
            pltpu.VMEM((128, NQ), F32),
            pltpu.VMEM((128, 8, 128), F32),
            dma((1,)),
            dma((4,)),
            dma((4,)),
            dma((16, 3)),
            dma((16, 3)),
            dma((4,)),
            dma((4,)),
            dma((8,)),
            dma((16,)),
            dma((4,)),
            dma((4,)),
            dma((16,)),
            dma((16,)),
        ],
        compiler_params=pltpu.CompilerParams(
            collective_id=0, has_side_effects=True, vmem_limit_bytes=56 * 1024 * 1024
        ),
    )(
        lengths,
        limits,
        kv_cache.reshape(2, 2, 512, 128),
        prefill_q,
        decode_q.reshape(8, 4, 16, 128),
        decode_kv.reshape(8, 16, 128),
    )
    return prefill_out, decode_out.reshape(decode_q.shape)


def solution(mesh):
    in_specs = (
        P("head", None, "ctx", "rep", None),
        P("head", "ctx", "rep", None),
        P(None, ("ctx", "rep"), None, "head", None),
        P(None, ("ctx", "rep"), None, None, "head", None),
        P(),
        P(None, ("ctx", "rep")),
    )
    out_specs = (P("head", "ctx", "rep", None), P(None, ("ctx", "rep"), None, "head", None))
    return jax.shard_map(
        on_device, mesh=mesh, in_specs=in_specs, out_specs=out_specs, check_vma=False
    )
```

```python
import functools
import math

import jax
import jax.numpy as jnp
from jax import lax
from jax.experimental import pallas as pl
from jax.experimental.pallas import tpu as pltpu
from jax.sharding import PartitionSpec as P

MESH = pl.DeviceIdType.MESH
NEG_FILL = -1e30
F32 = jnp.float32
BF16 = jnp.bfloat16
CHIPS = 8
NQ = 1024
HALF = 512
BLK = 256
QC = 512
PIECES = 2
PIECE = BLK // PIECES
AHEAD = 1


def split2(x):
    hi = x.astype(BF16)
    return hi, (x - hi.astype(F32)).astype(BF16)


def split3(x):
    hi = x.astype(BF16)
    rest = x - hi.astype(F32)
    mid = rest.astype(BF16)
    return hi, mid, (rest - mid.astype(F32)).astype(BF16)


def key_terms(k):
    hi, mid, lo = split3(k)
    return jnp.concatenate([hi, hi, mid, mid, hi, lo], axis=1)


def query_terms(q):
    hi, mid, lo = split3(q)
    return jnp.concatenate([hi, mid, hi, mid, lo, hi], axis=1)


def value_terms(v):
    hi, lo = split2(v.T)
    return jnp.concatenate([hi, lo], axis=0)


def dot_nt(a, b):
    return lax.dot_general(a, b, (((1,), (1,)), ((), ())), preferred_element_type=F32)


def weighted(v2, p):
    hi, lo = split2(p)
    both = jnp.dot(v2, hi, preferred_element_type=F32) + jnp.dot(v2, lo, preferred_element_type=F32)
    return both[:128] + both[128:]


def kernel(
    scale,
    span,
    len_ref,
    rl_ref,
    kv_ref,
    pq_ref,
    dq_ref,
    dkv_ref,
    po_ref,
    do_ref,
    raw,
    sendb,
    kvb,
    dkv,
    dsend,
    rlb,
    rq,
    rd,
    rr,
    qb,
    lb,
    db,
    q6,
    k6,
    v2b,
    lim,
    m_ref,
    l_ref,
    acc,
    ob,
    sem_local,
    sem_y_s,
    sem_y_r,
    sem_pq_s,
    sem_pq_r,
    sem_dq_s,
    sem_dq_r,
    sem_kp_s,
    sem_kf_s,
    sem_kx_s,
    sem_k_r,
    sem_po_s,
    sem_po_r,
    sem_do_s,
    sem_do_r,
):
    c = lax.axis_index("ctx")
    y = lax.axis_index("head")
    x = lax.axis_index("rep")
    z = c // 2
    core = c % 2

    def dest(t):
        even = (z + t) % 2 == 0
        return lax.rem(jnp.where(even, z + t, z - t + CHIPS), CHIPS)

    def source_of(chip, t):
        return lax.rem(jnp.where(chip % 2 == 0, chip - t + CHIPS, chip + t), CHIPS)

    mate = z + 1 - 2 * (z % 2)
    pair = z // 2
    own_i = pair // 2
    own_j = pair % 2
    diag = x == y

    load = pltpu.make_async_copy(kv_ref, raw, sem_local.at[0])
    load.start()
    load_d = pltpu.make_async_copy(dkv_ref, dkv, sem_local.at[1])
    load_d.start()

    barrier = pltpu.get_barrier_semaphore()

    def greet(ctx, head, rep):
        pl.semaphore_signal(barrier, inc=1, device_id=(ctx, head, rep), device_id_type=MESH)

    greet(2 * z + 1 - core, y, x)
    greet(2 * mate + core, y, x)
    for step in range(1, 4):
        greet(c, lax.rem(y + step, 4), x)
    count = 5
    for t in range(4):
        to_c = 2 * dest(t) + core
        from_c = 2 * source_of(z, t) + core
        for g in range(4):
            if t:
                greet(to_c, y, g)
                greet(from_c, y, g)
                greet(to_c, g, y)
                greet(from_c, x, g)
                count += 4
            else:

                @pl.when(x != g)
                def _():
                    greet(to_c, y, g)

                @pl.when(jnp.logical_not((y == g) & diag))
                def _():
                    greet(to_c, g, y)
                    greet(from_c, x, g)

    count = count + 3 + jnp.where(diag, 6, 8)

    for req in range(8):
        rlb[req] = jnp.full((1, 128), rl_ref[req, 0], jnp.int32)
    load_d.wait()
    for j in range(2):
        dsend[:, j] = dkv[pl.ds(j, 64, stride=2), :].reshape(8, 8, 128)
    load.wait()
    for i in range(2):
        for s in range(2):
            for j in range(2):
                sendb[2 * i + j, s] = raw[i, s, pl.ds(j, BLK, stride=2), :]

    pl.semaphore_wait(barrier, count)

    def y_copies(g):
        reqs = pl.ds(2 * g, 2)
        return [
            pltpu.make_async_remote_copy(
                src,
                dst,
                sem_y_s.at[g, n],
                sem_y_r.at[y, n],
                device_id=(c, g, x),
                device_id_type=MESH,
            )
            for n, (src, dst) in enumerate(
                ((dq_ref.at[reqs], rq.at[y]), (dsend.at[reqs], rd.at[y]), (rlb.at[reqs], rr.at[y]))
            )
        ]

    def y_keep():
        reqs = pl.ds(pl.multiple_of(2 * y, 2), 2)
        return [
            pltpu.make_async_copy(src, dst, sem_y_r.at[y, n])
            for n, (src, dst) in enumerate(
                ((dq_ref.at[reqs], rq.at[y]), (dsend.at[reqs], rd.at[y]), (rlb.at[reqs], rr.at[y]))
            )
        ]

    def pq_copy(t):
        zt = dest(t)
        p = zt // 2
        src = pq_ref.at[p // 2, :, pl.ds(pl.multiple_of(8 * (p % 2), 8), 8), :]
        dst = qb.at[pl.ds(16 * t, 16)]
        if t == 0:
            return pltpu.make_async_copy(src, dst, sem_pq_r.at[0])
        return pltpu.make_async_remote_copy(
            src, dst, sem_pq_s.at[t], sem_pq_r.at[t], device_id=(2 * zt + core, y, x), device_id_type=MESH
        )

    def dq_parts(t, h):
        p = dest(t) // 2
        i, j = p // 2, p % 2
        slot = 4 * t + x
        return (
            (rq.at[h, i, :, pl.ds(pl.multiple_of(8 * j, 8), 8), :], qb.at[pl.ds(64 + 4 * slot, 4)]),
            (rd.at[h, i, j], db.at[slot]),
            (rr.at[h, i], lb.at[slot]),
        )

    def dq_remote(t, h, n, part):
        return pltpu.make_async_remote_copy(
            part[0],
            part[1],
            sem_dq_s.at[4 * t + h, n],
            sem_dq_r.at[4 * t + x, n],
            device_id=(2 * dest(t) + core, y, h),
            device_id_type=MESH,
        )

    def dq_start(t, h):
        for n, part in enumerate(dq_parts(t, h)):
            if t:
                dq_remote(t, h, n, part).start()
            else:

                @pl.when(x == h)
                def _():
                    pltpu.make_async_copy(part[0], part[1], sem_dq_r.at[4 * t + x, n]).start()

                @pl.when(x != h)
                def _():
                    dq_remote(t, h, n, part).start()

    def dq_wait_send(t, h):
        for n, part in enumerate(dq_parts(t, h)):
            if t:
                dq_remote(t, h, n, part).wait_send()
            else:

                @pl.when(x != h)
                def _():
                    dq_remote(t, h, n, part).wait_send()

    def piece(h):
        return pl.ds(PIECE * h, PIECE)

    def kv_primary(t, h):
        zt = dest(t)
        return pltpu.make_async_remote_copy(
            sendb.at[zt // 2, :, piece(h)],
            kvb.at[t, :, piece(h)],
            sem_kp_s.at[t, h],
            sem_k_r.at[t, h],
            device_id=(2 * zt + core, y, x),
            device_id_type=MESH,
        )

    def kv_forward(t, h):
        return pltpu.make_async_remote_copy(
            kvb.at[t, :, piece(h)],
            kvb.at[t + 4, :, piece(h)],
            sem_kf_s.at[t, h],
            sem_k_r.at[t + 4, h],
            device_id=(2 * mate + core, y, x),
            device_id_type=MESH,
        )

    def kv_cross(u, h):
        return pltpu.make_async_remote_copy(
            kvb.at[u, :, piece(h)],
            kvb.at[u + 8, :, piece(h)],
            sem_kx_s.at[u, h],
            sem_k_r.at[u + 8, h],
            device_id=(2 * z + 1 - core, y, x),
            device_id_type=MESH,
        )

    def arrive(u):
        for h in range(PIECES):
            part = kvb.at[u, :, piece(h)]
            pltpu.make_async_copy(part, part, sem_k_r.at[u, h]).wait()

            @pl.when(u < 4)
            def _():
                kv_forward(u, h).start()

            kv_cross(u, h).start()

    def crossed(u):
        for h in range(PIECES):
            part = kvb.at[u, :, piece(h)]
            pltpu.make_async_copy(part, part, sem_k_r.at[u, h]).wait()

    for h in range(PIECES):
        pltpu.make_async_copy(sendb.at[pair, :, piece(h)], kvb.at[0, :, piece(h)], sem_k_r.at[0, h]).start()
    for g in range(4):

        @pl.when(y == g)
        def _():
            for copy in y_keep():
                copy.start()

        @pl.when(y != g)
        def _():
            for copy in y_copies(g):
                copy.start()

    for t in (3, 2, 1, 0):
        pq_copy(t).start()
    for t in (2, 1):
        for h in range(PIECES):
            kv_primary(t, h).start()

    arrive(jnp.int32(0))

    for g in range(4):
        for n, part in enumerate((rq.at[g], rd.at[g], rr.at[g])):
            pltpu.make_async_copy(part, part, sem_y_r.at[g, n]).wait()
        for t in (3, 2, 1, 0):
            dq_start(t, g)
    for h in range(PIECES):
        kv_primary(3, h).start()


    own_len = len_ref[2 * y + own_i]
    lane = lax.broadcasted_iota(jnp.int32, (1, 128), 1)
    for t in range(4):
        first = own_len - (span - 1) + 16 * (2 * source_of(z, t) + core)
        lim[:, pl.ds(128 * t, 128)] = first + lane // 8

    def own_slot(m):
        return jnp.where(m == 2, 4, jnp.where(m == 3, 2, jnp.where(m == 4, 3, m)))

    for m in range(1, AHEAD):
        arrive(own_slot(jnp.int32(m)))


    for t in range(4):
        part = qb.at[pl.ds(16 * t, 16)]
        pltpu.make_async_copy(part, part, sem_pq_r.at[t]).wait()

    @pl.loop(0, 16)
    def _(s):
        part = qb.at[pl.ds(64 + 4 * s, 4)]
        pltpu.make_async_copy(part, part, sem_dq_r.at[s, 0]).wait()
        pltpu.make_async_copy(db.at[s], db.at[s], sem_dq_r.at[s, 1]).wait()
        pltpu.make_async_copy(lb.at[s], lb.at[s], sem_dq_r.at[s, 2]).wait()

    for v in range(4):
        row = jnp.where(
            lane < 64,
            jnp.where(lane < 32, lb[4 * v], lb[4 * v + 1]),
            jnp.where(lane < 96, lb[4 * v + 2], lb[4 * v + 3]),
        )
        lim[:, pl.ds(HALF + 128 * v, 128)] = row

    @pl.loop(0, NQ // 128)
    def _(n):
        q = qb[pl.ds(16 * n, 16)].reshape(128, 128) * scale
        q6[pl.ds(pl.multiple_of(128 * n, 128), 128), :] = query_terms(q)

    m_ref[:, :HALF] = jnp.full((1, HALF), NEG_FILL, F32)
    l_ref[:, :HALF] = jnp.zeros((1, HALF), F32)
    acc[:, :HALF] = jnp.zeros((128, HALF), F32)
    drafts = db[...].reshape(64, 2, 128)
    s = dot_nt(key_terms(drafts[:, 0]), q6[pl.ds(HALF, HALF), :])
    key_id = lax.broadcasted_iota(jnp.int32, (64, HALF), 0)
    query_id = lax.broadcasted_iota(jnp.int32, (64, HALF), 1) // 8
    s = jnp.where((key_id // 4 == query_id // 4) & (key_id <= query_id), s, NEG_FILL)
    top = jnp.max(s, axis=0, keepdims=True)
    p = jnp.exp2(s - top)
    m_ref[:, HALF:] = top
    l_ref[:, HALF:] = jnp.sum(p, axis=0, keepdims=True)
    acc[:, HALF:] = weighted(value_terms(drafts[:, 1]), p)

    @pl.loop(0, 8)
    def _(m):
        u = own_slot(m)

        @pl.when(m + AHEAD < 8)
        def _():
            arrive(own_slot(m + AHEAD))

        crossed(u + 8)
        first = 2 * BLK * source_of(jnp.where(u < 4, z, mate), u % 4)
        for k in range(2):
            owner = core if k == 0 else 1 - core
            k6[owner] = key_terms(kvb[u + 8 * k, 0])
            v2b[owner] = value_terms(kvb[u + 8 * k, 1])
        for qc in range(NQ // QC):
            cols = pl.ds(QC * qc, QC)
            s = dot_nt(k6[...].reshape(2 * BLK, 768), q6[pl.ds(QC * qc, QC), :])
            place = lax.broadcasted_iota(jnp.int32, (2 * BLK, QC), 0)
            s = jnp.where(place < lim[:, cols] - first, s, NEG_FILL)
            old = m_ref[:, cols]
            top = jnp.maximum(old, jnp.max(s, axis=0, keepdims=True))
            fade = jnp.exp2(old - top)
            p = jnp.exp2(s - top)
            m_ref[:, cols] = top
            l_ref[:, cols] = l_ref[:, cols] * fade + jnp.sum(p, axis=0, keepdims=True)
            values = jnp.concatenate([v2b[0], v2b[1]], axis=1)
            acc[:, cols] = acc[:, cols] * fade + weighted(values, p)

    rows_j = pl.ds(pl.multiple_of(8 * own_j, 8), 8)

    def po_copy(t):
        src = ob.at[pl.ds(16 * t, 16)]
        dst = po_ref.at[own_i, :, rows_j, :]
        if t == 0:
            return pltpu.make_async_copy(src, dst, sem_po_r.at[0])
        return pltpu.make_async_remote_copy(
            src,
            dst,
            sem_po_s.at[t],
            sem_po_r.at[t],
            device_id=(2 * source_of(z, t) + core, y, x),
            device_id_type=MESH,
        )

    def do_ends(t, r):
        return ob.at[pl.ds(64 + 16 * t + 4 * r, 4)], do_ref.at[2 * y + own_i, :, rows_j, :]

    def do_remote(t, r):
        src, dst = do_ends(t, r)
        return pltpu.make_async_remote_copy(
            src,
            dst,
            sem_do_s.at[4 * t + r],
            sem_do_r.at[4 * t + y],
            device_id=(2 * source_of(z, t) + core, x, r),
            device_id_type=MESH,
        )

    def do_start(t, r):
        if t:
            do_remote(t, r).start()
            return
        mine = (x == r) & diag

        @pl.when(mine)
        def _():
            src, dst = do_ends(t, r)
            pltpu.make_async_copy(src, dst, sem_do_r.at[4 * t + y]).start()

        @pl.when(jnp.logical_not(mine))
        def _():
            do_remote(t, r).start()

    for qc in (3, 1, 2, 0):
        cols = pl.ds(256 * qc, 256)
        out = acc[:, cols] * (1.0 / l_ref[:, cols])
        ob[pl.ds(32 * qc, 32)] = out.T.reshape(32, 8, 128)
        for t in (2 * (qc % 2) + 1, 2 * (qc % 2)):
            if qc < 2:
                po_copy(t).start()
            else:
                for r in range(4):
                    do_start(t, r)

    for g in range(4):

        @pl.when(y != g)
        def _():
            for copy in y_copies(g):
                copy.wait_send()

    for t in range(1, 4):
        pq_copy(t).wait_send()
    for t in range(4):
        for g in range(4):
            dq_wait_send(t, g)
        for h in range(PIECES):
            if t:
                kv_primary(t, h).wait_send()
            kv_forward(t, h).wait_send()
    for u in range(8):
        for h in range(PIECES):
            kv_cross(u, h).wait_send()
    for t in range(4):
        if t:
            po_copy(t).wait_send()
        p = dest(t) // 2
        rows = pl.ds(pl.multiple_of(8 * (p % 2), 8), 8)
        got = po_ref.at[p // 2, :, rows, :]
        pltpu.make_async_copy(got, got, sem_po_r.at[t]).wait()
        for g in range(4):
            if t:
                do_remote(t, g).wait_send()
            else:

                @pl.when(jnp.logical_not((x == g) & diag))
                def _():
                    do_remote(t, g).wait_send()

            got = do_ref.at[2 * g + p // 2, :, rows, :]
            pltpu.make_async_copy(got, got, sem_do_r.at[4 * t + g]).wait()


def on_device(kv_cache, prefill_q, decode_q, decode_kv, lengths, row_length):
    head_dim = prefill_q.shape[-1]
    span = prefill_q.shape[1] * lax.axis_size("ctx")
    scale = math.log2(math.e) / math.sqrt(head_dim)
    hbm = pl.BlockSpec(memory_space=pltpu.MemorySpace.HBM)
    dma = pltpu.SemaphoreType.DMA
    prefill_out, decode_out = pl.pallas_call(
        functools.partial(kernel, scale, span),
        out_shape=(
            jax.ShapeDtypeStruct((2, 16, 16, 128), F32),
            jax.ShapeDtypeStruct((8, 4, 16, 128), F32),
        ),
        in_specs=[pl.BlockSpec(memory_space=pltpu.SMEM)] * 2 + [hbm] * 4,
        out_specs=(hbm, hbm),
        scratch_shapes=[
            pltpu.VMEM((2, 2, 512, 128), F32),
            pltpu.VMEM((4, 2, BLK, 128), F32),
            pltpu.VMEM((16, 2, BLK, 128), F32),
            pltpu.VMEM((128, 128), F32),
            pltpu.VMEM((8, 2, 8, 128), F32),
            pltpu.VMEM((8, 1, 128), jnp.int32),
            pltpu.VMEM((4, 2, 4, 16, 128), F32),
            pltpu.VMEM((4, 2, 2, 8, 128), F32),
            pltpu.VMEM((4, 2, 1, 128), jnp.int32),
            pltpu.VMEM((128, 8, 128), F32),
            pltpu.VMEM((16, 1, 128), jnp.int32),
            pltpu.VMEM((16, 8, 128), F32),
            pltpu.VMEM((NQ, 768), BF16),
            pltpu.VMEM((2, BLK, 768), BF16),
            pltpu.VMEM((2, 256, BLK), BF16),
            pltpu.VMEM((1, NQ), jnp.int32),
            pltpu.VMEM((1, NQ), F32),
            pltpu.VMEM((1, NQ), F32),
            pltpu.VMEM((128, NQ), F32),
            pltpu.VMEM((128, 8, 128), F32),
            dma((2,)),
            dma((4, 3)),
            dma((4, 3)),
            dma((4,)),
            dma((4,)),
            dma((16, 3)),
            dma((16, 3)),
            dma((4, PIECES)),
            dma((4, PIECES)),
            dma((8, PIECES)),
            dma((16, PIECES)),
            dma((4,)),
            dma((4,)),
            dma((16,)),
            dma((16,)),
        ],
        compiler_params=pltpu.CompilerParams(
            collective_id=0, has_side_effects=True, vmem_limit_bytes=56 * 1024 * 1024
        ),
    )(
        lengths,
        row_length,
        kv_cache.reshape(2, 2, 512, 128),
        prefill_q,
        decode_q.reshape(8, 4, 16, 128),
        decode_kv.reshape(128, 128),
    )
    return prefill_out, decode_out.reshape(decode_q.shape)


def solution(mesh):
    in_specs = (
        P("head", None, "ctx", "rep", None),
        P("head", "ctx", "rep", None),
        P(None, ("ctx", "rep"), None, "head", None),
        P(None, ("ctx", "rep"), None, None, "head", None),
        P(),
        P(None, ("ctx", "rep")),
    )
    out_specs = (P("head", "ctx", "rep", None), P(None, ("ctx", "rep"), None, "head", None))
    return jax.shard_map(
        on_device, mesh=mesh, in_specs=in_specs, out_specs=out_specs, check_vma=False
    )
```

```python
import functools
import math

import jax
import jax.numpy as jnp
from jax import lax
from jax.experimental import pallas as pl
from jax.experimental.pallas import tpu as pltpu
from jax.sharding import PartitionSpec as P

MESH = pl.DeviceIdType.MESH
NEG_FILL = -1e30
F32 = jnp.float32
BF16 = jnp.bfloat16
CHIPS = 8
NQ = 1024
HALF = 512
BLK = 256
QC = 512
PIECES = 2
PIECE = BLK // PIECES
OWN = (0, 1, 4, 2, 3, 5, 6, 7)
AHEAD = 1
PLAN = (
    ("y", 0),
    ("keep", 0),
    ("prefill", 1),
    ("prefill", 0),
    ("hear", 0),
    ("tell", 1),
    ("prefill", 2),
    ("hear", 1),
    ("tell", 2),
    ("prefill", 3),
    ("relay", 0),
    ("decode", 1),
    ("hear", 2),
    ("decode", 3),
    ("decode", 2),
    ("decode", 0),
    ("keys", (1, 0)),
    ("arrive", (0, 0)),
    ("keys", (1, 1)),
    ("arrive", (0, 1)),
    ("keys", (2, 0)),
    ("keys", (2, 1)),
    ("keys", (3, 0)),
    ("keys", (3, 1)),
    ("arrive", (1, 0)),
)
LAST = max(PIECES * which[0] + which[1] for what, which in PLAN if what == "arrive")


def split2(x):
    hi = x.astype(BF16)
    return hi, (x - hi.astype(F32)).astype(BF16)


def split3(x):
    hi = x.astype(BF16)
    rest = x - hi.astype(F32)
    mid = rest.astype(BF16)
    return hi, mid, (rest - mid.astype(F32)).astype(BF16)


def key_terms(k):
    hi, mid, lo = split3(k)
    return jnp.concatenate([hi, hi, mid, mid, hi, lo], axis=1)


def query_terms(q):
    hi, mid, lo = split3(q)
    return jnp.concatenate([hi, mid, hi, mid, lo, hi], axis=1)


def value_terms(v):
    hi, lo = split2(v.T)
    return jnp.concatenate([hi, lo], axis=0)


def dot_nt(a, b):
    return lax.dot_general(a, b, (((1,), (1,)), ((), ())), preferred_element_type=F32)


def weighted(v2, p):
    hi, lo = split2(p)
    both = jnp.dot(v2, hi, preferred_element_type=F32) + jnp.dot(v2, lo, preferred_element_type=F32)
    return both[:128] + both[128:]


def kernel(
    scale,
    span,
    len_ref,
    rl_ref,
    kv_ref,
    pq_ref,
    dq_ref,
    dkv_ref,
    po_ref,
    do_ref,
    raw,
    sendb,
    kvb,
    dkv,
    dsend,
    rlb,
    rq,
    rd,
    rr,
    qb,
    lb,
    db,
    q6,
    k6,
    v2b,
    lim,
    m_ref,
    l_ref,
    acc,
    ob,
    sem_local,
    near,
    sem_y_s,
    sem_y_r,
    sem_pq_s,
    sem_pq_r,
    sem_dq_s,
    sem_dq_r,
    sem_kp_s,
    sem_kf_s,
    sem_kx_s,
    sem_k_r,
    sem_po_s,
    sem_po_r,
    sem_do_s,
    sem_do_r,
):
    c = lax.axis_index("ctx")
    y = lax.axis_index("head")
    x = lax.axis_index("rep")
    z = c // 2
    core = c % 2

    def dest(t):
        even = (z + t) % 2 == 0
        return lax.rem(jnp.where(even, z + t, z - t + CHIPS), CHIPS)

    def source_of(chip, t):
        return lax.rem(jnp.where(chip % 2 == 0, chip - t + CHIPS, chip + t), CHIPS)

    mate = z + 1 - 2 * (z % 2)
    pair = z // 2
    own_i = pair // 2
    own_j = pair % 2
    diag = x == y

    load = pltpu.make_async_copy(kv_ref, raw, sem_local.at[0])
    load.start()
    load_d = pltpu.make_async_copy(dkv_ref, dkv, sem_local.at[1])
    load_d.start()

    barrier = pltpu.get_barrier_semaphore()

    def greet(ctx, head, rep):
        pl.semaphore_signal(barrier, inc=1, device_id=(ctx, head, rep), device_id_type=MESH)

    up = 2 * lax.rem(z + 1, CHIPS) + core
    down = 2 * lax.rem(z + CHIPS - 1, CHIPS) + core
    greet(2 * z + 1 - core, y, x)
    greet(up, y, x)
    greet(down, y, x)
    for step in range(1, 4):
        greet(c, lax.rem(y + step, 4), x)
        greet(c, y, lax.rem(x + step, 4))

    for req in range(8):
        rlb[req] = jnp.full((1, 128), rl_ref[req], jnp.int32)
    load_d.wait()
    for j in range(2):
        dsend[:, j] = dkv[pl.ds(j, 64, stride=2), :].reshape(8, 8, 128)
    load.wait()
    for i in range(2):
        for s in range(2):
            for j in range(2):
                sendb[2 * i + j, s] = raw[i, s, pl.ds(j, BLK, stride=2), :]

    pl.semaphore_wait(barrier, 9)

    def tell(n):
        for there in (up, down):
            pl.semaphore_signal(near.at[n], inc=1, device_id=(there, y, x), device_id_type=MESH)

    def hear(n):
        pl.semaphore_wait(near.at[n], 2)

    tell(0)

    def y_copies(g):
        reqs = pl.ds(2 * g, 2)
        return [
            pltpu.make_async_remote_copy(
                src,
                dst,
                sem_y_s.at[g, n],
                sem_y_r.at[y, n],
                device_id=(c, g, x),
                device_id_type=MESH,
            )
            for n, (src, dst) in enumerate(
                ((dq_ref.at[reqs], rq.at[y]), (dsend.at[reqs], rd.at[y]), (rlb.at[reqs], rr.at[y]))
            )
        ]

    def y_keep():
        reqs = pl.ds(pl.multiple_of(2 * y, 2), 2)
        return [
            pltpu.make_async_copy(src, dst, sem_y_r.at[y, n])
            for n, (src, dst) in enumerate(
                ((dq_ref.at[reqs], rq.at[y]), (dsend.at[reqs], rd.at[y]), (rlb.at[reqs], rr.at[y]))
            )
        ]

    def pq_copy(t):
        zt = dest(t)
        p = zt // 2
        src = pq_ref.at[p // 2, :, pl.ds(pl.multiple_of(8 * (p % 2), 8), 8), :]
        dst = qb.at[pl.ds(16 * t, 16)]
        if t == 0:
            return pltpu.make_async_copy(src, dst, sem_pq_r.at[0])
        return pltpu.make_async_remote_copy(
            src, dst, sem_pq_s.at[t], sem_pq_r.at[t], device_id=(2 * zt + core, y, x), device_id_type=MESH
        )

    def dq_parts(t, h):
        p = dest(t) // 2
        i, j = p // 2, p % 2
        slot = 4 * t + x
        return (
            (rq.at[h, i, :, pl.ds(pl.multiple_of(8 * j, 8), 8), :], qb.at[pl.ds(64 + 4 * slot, 4)]),
            (rd.at[h, i, j], db.at[slot]),
            (rr.at[h, i], lb.at[slot]),
        )

    def dq_remote(t, h, n, part):
        return pltpu.make_async_remote_copy(
            part[0],
            part[1],
            sem_dq_s.at[4 * t + h, n],
            sem_dq_r.at[4 * t + x, n],
            device_id=(2 * dest(t) + core, y, h),
            device_id_type=MESH,
        )

    def dq_start(t, h):
        for n, part in enumerate(dq_parts(t, h)):
            if t:
                dq_remote(t, h, n, part).start()
            else:

                @pl.when(x == h)
                def _():
                    pltpu.make_async_copy(part[0], part[1], sem_dq_r.at[4 * t + x, n]).start()

                @pl.when(x != h)
                def _():
                    dq_remote(t, h, n, part).start()

    def dq_wait_send(t, h):
        for n, part in enumerate(dq_parts(t, h)):
            if t:
                dq_remote(t, h, n, part).wait_send()
            else:

                @pl.when(x != h)
                def _():
                    dq_remote(t, h, n, part).wait_send()

    def piece(h):
        return pl.ds(PIECE * h, PIECE)

    def kv_primary(t, h):
        zt = dest(t)
        return pltpu.make_async_remote_copy(
            sendb.at[zt // 2, :, piece(h)],
            kvb.at[t, :, piece(h)],
            sem_kp_s.at[t, h],
            sem_k_r.at[t, h],
            device_id=(2 * zt + core, y, x),
            device_id_type=MESH,
        )

    def kv_forward(t, h):
        return pltpu.make_async_remote_copy(
            kvb.at[t, :, piece(h)],
            kvb.at[t + 4, :, piece(h)],
            sem_kf_s.at[t, h],
            sem_k_r.at[t + 4, h],
            device_id=(2 * mate + core, y, x),
            device_id_type=MESH,
        )

    def kv_cross(u, h):
        return pltpu.make_async_remote_copy(
            kvb.at[u, :, piece(h)],
            kvb.at[u + 8, :, piece(h)],
            sem_kx_s.at[u, h],
            sem_k_r.at[u + 8, h],
            device_id=(2 * z + 1 - core, y, x),
            device_id_type=MESH,
        )

    def arrive(u, h):
        part = kvb.at[u, :, piece(h)]
        pltpu.make_async_copy(part, part, sem_k_r.at[u, h]).wait()

        @pl.when(u < 4)
        def _():
            kv_forward(u, h).start()

        kv_cross(u, h).start()

    def crossed(u):
        for h in range(PIECES):
            part = kvb.at[u, :, piece(h)]
            pltpu.make_async_copy(part, part, sem_k_r.at[u, h]).wait()

    def along_y():
        for g in range(4):

            @pl.when(y == g)
            def _():
                for copy in y_keep():
                    copy.start()

            @pl.when(y != g)
            def _():
                for copy in y_copies(g):
                    copy.start()

    def along_y_done():
        for g in range(4):
            for n, part in enumerate((rq.at[g], rd.at[g], rr.at[g])):
                pltpu.make_async_copy(part, part, sem_y_r.at[g, n]).wait()

    def own_slot(m):
        slot = OWN[-1]
        for place, value in enumerate(OWN[:-1]):
            slot = jnp.where(m == place, value, slot)
        return slot

    for what, which in PLAN:
        if what == "hear":
            hear(which)
        elif what == "tell":
            tell(which)
        elif what == "y":
            along_y()
        elif what == "relay":
            along_y_done()
        elif what == "prefill":
            pq_copy(which).start()
        elif what == "decode":
            for g in range(4):
                dq_start(which, g)
        elif what == "keys":
            kv_primary(*which).start()
        elif what == "keep":
            for h in range(PIECES):
                src, dst = sendb.at[pair, :, piece(h)], kvb.at[0, :, piece(h)]
                pltpu.make_async_copy(src, dst, sem_k_r.at[0, h]).start()
        elif what == "arrive":
            arrive(jnp.int32(OWN[which[0]]), which[1])

    own_len = len_ref[2 * y + own_i]
    lane = lax.broadcasted_iota(jnp.int32, (1, 128), 1)
    for t in range(4):
        first = own_len - (span - 1) + 16 * (2 * source_of(z, t) + core)
        lim[:, pl.ds(128 * t, 128)] = first + lane // 8

    for t in range(4):
        part = qb.at[pl.ds(16 * t, 16)]
        pltpu.make_async_copy(part, part, sem_pq_r.at[t]).wait()

    @pl.loop(0, 16)
    def _(s):
        part = qb.at[pl.ds(64 + 4 * s, 4)]
        pltpu.make_async_copy(part, part, sem_dq_r.at[s, 0]).wait()
        pltpu.make_async_copy(db.at[s], db.at[s], sem_dq_r.at[s, 1]).wait()
        pltpu.make_async_copy(lb.at[s], lb.at[s], sem_dq_r.at[s, 2]).wait()

    for v in range(4):
        row = jnp.where(
            lane < 64,
            jnp.where(lane < 32, lb[4 * v], lb[4 * v + 1]),
            jnp.where(lane < 96, lb[4 * v + 2], lb[4 * v + 3]),
        )
        lim[:, pl.ds(HALF + 128 * v, 128)] = row

    @pl.loop(0, NQ // 128)
    def _(n):
        q = qb[pl.ds(16 * n, 16)].reshape(128, 128) * scale
        q6[pl.ds(pl.multiple_of(128 * n, 128), 128), :] = query_terms(q)

    m_ref[:, :HALF] = jnp.full((1, HALF), NEG_FILL, F32)
    l_ref[:, :HALF] = jnp.zeros((1, HALF), F32)
    acc[:, :HALF] = jnp.zeros((128, HALF), F32)
    drafts = db[...].reshape(64, 2, 128)
    s = dot_nt(key_terms(drafts[:, 0]), q6[pl.ds(HALF, HALF), :])
    key_id = lax.broadcasted_iota(jnp.int32, (64, HALF), 0)
    query_id = lax.broadcasted_iota(jnp.int32, (64, HALF), 1) // 8
    s = jnp.where((key_id // 4 == query_id // 4) & (key_id <= query_id), s, NEG_FILL)
    top = jnp.max(s, axis=0, keepdims=True)
    p = jnp.exp2(s - top)
    m_ref[:, HALF:] = top
    l_ref[:, HALF:] = jnp.sum(p, axis=0, keepdims=True)
    acc[:, HALF:] = weighted(value_terms(drafts[:, 1]), p)

    @pl.loop(0, 8)
    def _(m):
        u = own_slot(m)

        for h in range(PIECES):

            @pl.when((m + AHEAD < 8) & (PIECES * (m + AHEAD) + h > LAST))
            def _():
                arrive(own_slot(m + AHEAD), h)

        crossed(u + 8)
        first = 2 * BLK * source_of(jnp.where(u < 4, z, mate), u % 4)
        for k in range(2):
            owner = core if k == 0 else 1 - core
            k6[owner] = key_terms(kvb[u + 8 * k, 0])
            v2b[owner] = value_terms(kvb[u + 8 * k, 1])
        for qc in range(NQ // QC):
            cols = pl.ds(QC * qc, QC)
            s = dot_nt(k6[...].reshape(2 * BLK, 768), q6[pl.ds(QC * qc, QC), :])
            place = lax.broadcasted_iota(jnp.int32, (2 * BLK, QC), 0)
            s = jnp.where(place < lim[:, cols] - first, s, NEG_FILL)
            old = m_ref[:, cols]
            top = jnp.maximum(old, jnp.max(s, axis=0, keepdims=True))
            fade = jnp.exp2(old - top)
            p = jnp.exp2(s - top)
            m_ref[:, cols] = top
            l_ref[:, cols] = l_ref[:, cols] * fade + jnp.sum(p, axis=0, keepdims=True)
            values = jnp.concatenate([v2b[0], v2b[1]], axis=1)
            acc[:, cols] = acc[:, cols] * fade + weighted(values, p)

    rows_j = pl.ds(pl.multiple_of(8 * own_j, 8), 8)

    def po_copy(t):
        src = ob.at[pl.ds(16 * t, 16)]
        dst = po_ref.at[own_i, :, rows_j, :]
        if t == 0:
            return pltpu.make_async_copy(src, dst, sem_po_r.at[0])
        return pltpu.make_async_remote_copy(
            src,
            dst,
            sem_po_s.at[t],
            sem_po_r.at[t],
            device_id=(2 * source_of(z, t) + core, y, x),
            device_id_type=MESH,
        )

    def do_ends(t, r):
        return ob.at[pl.ds(64 + 16 * t + 4 * r, 4)], do_ref.at[2 * y + own_i, :, rows_j, :]

    def do_remote(t, r):
        src, dst = do_ends(t, r)
        return pltpu.make_async_remote_copy(
            src,
            dst,
            sem_do_s.at[4 * t + r],
            sem_do_r.at[4 * t + y],
            device_id=(2 * source_of(z, t) + core, x, r),
            device_id_type=MESH,
        )

    def do_start(t, r):
        if t:
            do_remote(t, r).start()
            return
        mine = (x == r) & diag

        @pl.when(mine)
        def _():
            src, dst = do_ends(t, r)
            pltpu.make_async_copy(src, dst, sem_do_r.at[4 * t + y]).start()

        @pl.when(jnp.logical_not(mine))
        def _():
            do_remote(t, r).start()

    for qc in (3, 1, 2, 0):
        cols = pl.ds(256 * qc, 256)
        out = acc[:, cols] * (1.0 / l_ref[:, cols])
        ob[pl.ds(32 * qc, 32)] = out.T.reshape(32, 8, 128)
        for t in (2 * (qc % 2) + 1, 2 * (qc % 2)):
            if qc < 2:
                po_copy(t).start()
            else:
                for r in range(4):
                    do_start(t, r)

    for g in range(4):

        @pl.when(y != g)
        def _():
            for copy in y_copies(g):
                copy.wait_send()

    for t in range(1, 4):
        pq_copy(t).wait_send()
    for t in range(4):
        for g in range(4):
            dq_wait_send(t, g)
        for h in range(PIECES):
            if t:
                kv_primary(t, h).wait_send()
            kv_forward(t, h).wait_send()
    for u in range(8):
        for h in range(PIECES):
            kv_cross(u, h).wait_send()
    for t in range(4):
        if t:
            po_copy(t).wait_send()
        p = dest(t) // 2
        rows = pl.ds(pl.multiple_of(8 * (p % 2), 8), 8)
        got = po_ref.at[p // 2, :, rows, :]
        pltpu.make_async_copy(got, got, sem_po_r.at[t]).wait()
        for g in range(4):
            if t:
                do_remote(t, g).wait_send()
            else:

                @pl.when(jnp.logical_not((x == g) & diag))
                def _():
                    do_remote(t, g).wait_send()

            got = do_ref.at[2 * g + p // 2, :, rows, :]
            pltpu.make_async_copy(got, got, sem_do_r.at[4 * t + g]).wait()


def on_device(kv_cache, prefill_q, decode_q, decode_kv, lengths, row_length):
    head_dim = prefill_q.shape[-1]
    span = prefill_q.shape[1] * lax.axis_size("ctx")
    scale = math.log2(math.e) / math.sqrt(head_dim)
    hbm = pl.BlockSpec(memory_space=pltpu.MemorySpace.HBM)
    dma = pltpu.SemaphoreType.DMA
    prefill_out, decode_out = pl.pallas_call(
        functools.partial(kernel, scale, span),
        out_shape=(
            jax.ShapeDtypeStruct((2, 16, 16, 128), F32),
            jax.ShapeDtypeStruct((8, 4, 16, 128), F32),
        ),
        in_specs=[pl.BlockSpec(memory_space=pltpu.SMEM)] * 2 + [hbm] * 4,
        out_specs=(hbm, hbm),
        scratch_shapes=[
            pltpu.VMEM((2, 2, 512, 128), F32),
            pltpu.VMEM((4, 2, BLK, 128), F32),
            pltpu.VMEM((16, 2, BLK, 128), F32),
            pltpu.VMEM((128, 128), F32),
            pltpu.VMEM((8, 2, 8, 128), F32),
            pltpu.VMEM((8, 1, 128), jnp.int32),
            pltpu.VMEM((4, 2, 4, 16, 128), F32),
            pltpu.VMEM((4, 2, 2, 8, 128), F32),
            pltpu.VMEM((4, 2, 1, 128), jnp.int32),
            pltpu.VMEM((128, 8, 128), F32),
            pltpu.VMEM((16, 1, 128), jnp.int32),
            pltpu.VMEM((16, 8, 128), F32),
            pltpu.VMEM((NQ, 768), BF16),
            pltpu.VMEM((2, BLK, 768), BF16),
            pltpu.VMEM((2, 256, BLK), BF16),
            pltpu.VMEM((1, NQ), jnp.int32),
            pltpu.VMEM((1, NQ), F32),
            pltpu.VMEM((1, NQ), F32),
            pltpu.VMEM((128, NQ), F32),
            pltpu.VMEM((128, 8, 128), F32),
            dma((2,)),
            pltpu.SemaphoreType.REGULAR((3,)),
            dma((4, 3)),
            dma((4, 3)),
            dma((4,)),
            dma((4,)),
            dma((16, 3)),
            dma((16, 3)),
            dma((4, PIECES)),
            dma((4, PIECES)),
            dma((8, PIECES)),
            dma((16, PIECES)),
            dma((4,)),
            dma((4,)),
            dma((16,)),
            dma((16,)),
        ],
        compiler_params=pltpu.CompilerParams(
            collective_id=0, has_side_effects=True, vmem_limit_bytes=56 * 1024 * 1024
        ),
    )(
        lengths,
        row_length.reshape(8),
        kv_cache.reshape(2, 2, 512, 128),
        prefill_q,
        decode_q.reshape(8, 4, 16, 128),
        decode_kv.reshape(128, 128),
    )
    return prefill_out, decode_out.reshape(decode_q.shape)


def solution(mesh):
    in_specs = (
        P("head", None, "ctx", "rep", None),
        P("head", "ctx", "rep", None),
        P(None, ("ctx", "rep"), None, "head", None),
        P(None, ("ctx", "rep"), None, None, "head", None),
        P(),
        P(None, ("ctx", "rep")),
    )
    out_specs = (P("head", "ctx", "rep", None), P(None, ("ctx", "rep"), None, "head", None))
    return jax.shard_map(
        on_device, mesh=mesh, in_specs=in_specs, out_specs=out_specs, check_vma=False
    )
```

```python
import functools
import math

import jax
import jax.numpy as jnp
from jax import lax
from jax.experimental import pallas as pl
from jax.experimental.pallas import tpu as pltpu
from jax.sharding import PartitionSpec as P

MESH = pl.DeviceIdType.MESH
NEG_FILL = -1e30
F32 = jnp.float32
BF16 = jnp.bfloat16
CHIPS = 8
HALF = 512
BLK = 256
PIECES = 2
PIECE = BLK // PIECES
OWN = (0, 4, 1, 5, 3, 2, 7, 6)
SPOT = (1, 1)
PLAN = (
    ("y", 0),
    ("keep", 0),
    ("prefill", 1),
    ("prefill", 0),
    ("arrive", (0, 0)),
    ("hear", 0),
    ("tell", 1),
    ("prefill", 2),
    ("arrive", (0, 1)),
    ("hear", 1),
    ("tell", 2),
    ("prefill", 3),
    ("keys", (1, 0)),
    ("keys", (1, 1)),
    ("keys", (2, 0)),
    ("relay", 0),
    ("hear", 2),
    ("decode", 3),
    ("decode", 1),
    ("decode", 2),
    ("decode", 0),
    ("keys", (3, 0)),
    ("keys", (2, 1)),
    ("keys", (3, 1)),
    ("prefill queries", 0),
    ("ready", 0),
    ("attend", (0, 0)),
    ("arrive", (1, 0)),
    ("arrive", (1, 1)),
    ("ready", 1),
    ("attend", (1, 0)),
    ("arrive", (2, 0)),
    ("arrive", (2, 1)),
    ("ready", 2),
    ("attend", (2, 0)),
    ("arrive", (5, 0)),
    ("decode queries", 0),
    ("attend", (0, 1)),
    ("attend", (1, 1)),
    ("arrive", (3, 0)),
    ("arrive", (3, 1)),
    ("attend", (2, 1)),
    ("arrive", (4, 0)),
)
EARLY = 1 + max(which for what, which in PLAN if what == "ready")


def split2(x):
    hi = x.astype(BF16)
    return hi, (x - hi.astype(F32)).astype(BF16)


def split3(x):
    hi = x.astype(BF16)
    rest = x - hi.astype(F32)
    mid = rest.astype(BF16)
    return hi, mid, (rest - mid.astype(F32)).astype(BF16)


def key_terms(k):
    hi, mid, lo = split3(k)
    return jnp.concatenate([hi, hi, mid, mid, hi, lo], axis=1)


def query_terms(q):
    hi, mid, lo = split3(q)
    return jnp.concatenate([hi, mid, hi, mid, lo, hi], axis=1)


def value_terms(v):
    hi, lo = split2(v.T)
    return jnp.concatenate([hi, lo], axis=0)


def dot_nt(a, b):
    return lax.dot_general(a, b, (((1,), (1,)), ((), ())), preferred_element_type=F32)


def weighted(v2, p):
    hi, lo = split2(p)
    both = jnp.dot(v2, hi, preferred_element_type=F32) + jnp.dot(v2, lo, preferred_element_type=F32)
    return both[:128] + both[128:]


def kernel(
    scale,
    span,
    len_ref,
    rl_ref,
    kv_ref,
    pq_ref,
    dq_ref,
    dkv_ref,
    po_ref,
    do_ref,
    raw,
    sendb,
    kvb,
    dkv,
    dsend,
    rlb,
    rq,
    rd,
    rr,
    qb,
    lb,
    db,
    q6,
    k6,
    v2b,
    lim,
    m_ref,
    l_ref,
    acc,
    ob,
    sem_local,
    near,
    sem_y_s,
    sem_y_r,
    sem_pq_s,
    sem_pq_r,
    sem_dq_s,
    sem_dq_r,
    sem_kp_s,
    sem_kf_s,
    sem_kx_s,
    sem_k_r,
    sem_po_s,
    sem_po_r,
    sem_do_s,
    sem_do_r,
):
    c = lax.axis_index("ctx")
    y = lax.axis_index("head")
    x = lax.axis_index("rep")
    z = c // 2
    core = c % 2

    def dest(t):
        even = (z + t) % 2 == 0
        return lax.rem(jnp.where(even, z + t, z - t + CHIPS), CHIPS)

    def source_of(chip, t):
        return lax.rem(jnp.where(chip % 2 == 0, chip - t + CHIPS, chip + t), CHIPS)

    mate = z + 1 - 2 * (z % 2)
    pair = z // 2
    own_i = pair // 2
    own_j = pair % 2
    diag = x == y

    load = pltpu.make_async_copy(kv_ref, raw, sem_local.at[0])
    load.start()
    load_d = pltpu.make_async_copy(dkv_ref, dkv, sem_local.at[1])
    load_d.start()

    barrier = pltpu.get_barrier_semaphore()

    def greet(ctx, head, rep):
        pl.semaphore_signal(barrier, inc=1, device_id=(ctx, head, rep), device_id_type=MESH)

    up = 2 * lax.rem(z + 1, CHIPS) + core
    down = 2 * lax.rem(z + CHIPS - 1, CHIPS) + core
    greet(2 * z + 1 - core, y, x)
    greet(up, y, x)
    greet(down, y, x)
    for step in range(1, 4):
        greet(c, lax.rem(y + step, 4), x)
        greet(c, y, lax.rem(x + step, 4))

    for req in range(8):
        rlb[req] = jnp.full((1, 128), rl_ref[req], jnp.int32)
    load_d.wait()
    for j in range(2):
        dsend[:, j] = dkv[pl.ds(j, 64, stride=2), :].reshape(8, 8, 128)
    load.wait()
    for i in range(2):
        for s in range(2):
            for j in range(2):
                sendb[2 * i + j, s] = raw[i, s, pl.ds(j, BLK, stride=2), :]

    pl.semaphore_wait(barrier, 9)

    def tell(n):
        for there in (up, down):
            pl.semaphore_signal(near.at[n], inc=1, device_id=(there, y, x), device_id_type=MESH)

    def hear(n):
        pl.semaphore_wait(near.at[n], 2)

    tell(0)

    def y_copies(g):
        reqs = pl.ds(2 * g, 2)
        return [
            pltpu.make_async_remote_copy(
                src,
                dst,
                sem_y_s.at[g, n],
                sem_y_r.at[y, n],
                device_id=(c, g, x),
                device_id_type=MESH,
            )
            for n, (src, dst) in enumerate(
                ((dq_ref.at[reqs], rq.at[y]), (dsend.at[reqs], rd.at[y]), (rlb.at[reqs], rr.at[y]))
            )
        ]

    def y_keep():
        reqs = pl.ds(pl.multiple_of(2 * y, 2), 2)
        return [
            pltpu.make_async_copy(src, dst, sem_y_r.at[y, n])
            for n, (src, dst) in enumerate(
                ((dq_ref.at[reqs], rq.at[y]), (dsend.at[reqs], rd.at[y]), (rlb.at[reqs], rr.at[y]))
            )
        ]

    def pq_copy(t):
        zt = dest(t)
        p = zt // 2
        src = pq_ref.at[p // 2, :, pl.ds(pl.multiple_of(8 * (p % 2), 8), 8), :]
        dst = qb.at[pl.ds(16 * t, 16)]
        if t == 0:
            return pltpu.make_async_copy(src, dst, sem_pq_r.at[0])
        return pltpu.make_async_remote_copy(
            src, dst, sem_pq_s.at[t], sem_pq_r.at[t], device_id=(2 * zt + core, y, x), device_id_type=MESH
        )

    def dq_parts(t, h):
        p = dest(t) // 2
        i, j = p // 2, p % 2
        slot = 4 * t + x
        return (
            (rq.at[h, i, :, pl.ds(pl.multiple_of(8 * j, 8), 8), :], qb.at[pl.ds(64 + 4 * slot, 4)]),
            (rd.at[h, i, j], db.at[slot]),
            (rr.at[h, i], lb.at[slot]),
        )

    def dq_remote(t, h, n, part):
        return pltpu.make_async_remote_copy(
            part[0],
            part[1],
            sem_dq_s.at[4 * t + h, n],
            sem_dq_r.at[4 * t + x, n],
            device_id=(2 * dest(t) + core, y, h),
            device_id_type=MESH,
        )

    def dq_start(t, h):
        for n, part in enumerate(dq_parts(t, h)):
            if t:
                dq_remote(t, h, n, part).start()
            else:

                @pl.when(x == h)
                def _():
                    pltpu.make_async_copy(part[0], part[1], sem_dq_r.at[4 * t + x, n]).start()

                @pl.when(x != h)
                def _():
                    dq_remote(t, h, n, part).start()

    def dq_wait_send(t, h):
        for n, part in enumerate(dq_parts(t, h)):
            if t:
                dq_remote(t, h, n, part).wait_send()
            else:

                @pl.when(x != h)
                def _():
                    dq_remote(t, h, n, part).wait_send()

    def piece(h):
        return pl.ds(PIECE * h, PIECE)

    def kv_primary(t, h):
        zt = dest(t)
        return pltpu.make_async_remote_copy(
            sendb.at[zt // 2, :, piece(h)],
            kvb.at[t, :, piece(h)],
            sem_kp_s.at[t, h],
            sem_k_r.at[t, h],
            device_id=(2 * zt + core, y, x),
            device_id_type=MESH,
        )

    def kv_forward(t, h):
        return pltpu.make_async_remote_copy(
            kvb.at[t, :, piece(h)],
            kvb.at[t + 4, :, piece(h)],
            sem_kf_s.at[t, h],
            sem_k_r.at[t + 4, h],
            device_id=(2 * mate + core, y, x),
            device_id_type=MESH,
        )

    def kv_cross(u, h):
        return pltpu.make_async_remote_copy(
            kvb.at[u, :, piece(h)],
            kvb.at[u + 8, :, piece(h)],
            sem_kx_s.at[u, h],
            sem_k_r.at[u + 8, h],
            device_id=(2 * z + 1 - core, y, x),
            device_id_type=MESH,
        )

    def arrive(u, h):
        part = kvb.at[u, :, piece(h)]
        pltpu.make_async_copy(part, part, sem_k_r.at[u, h]).wait()

        @pl.when(u < 4)
        def _():
            kv_forward(u, h).start()

        kv_cross(u, h).start()

    def crossed(u):
        for h in range(PIECES):
            part = kvb.at[u, :, piece(h)]
            pltpu.make_async_copy(part, part, sem_k_r.at[u, h]).wait()

    def along_y():
        for g in range(4):

            @pl.when(y == g)
            def _():
                for copy in y_keep():
                    copy.start()

            @pl.when(y != g)
            def _():
                for copy in y_copies(g):
                    copy.start()

    def along_y_done():
        for g in range(4):
            for n, part in enumerate((rq.at[g], rd.at[g], rr.at[g])):
                pltpu.make_async_copy(part, part, sem_y_r.at[g, n]).wait()

    def own_slot(m):
        slot = OWN[-1]
        for place, value in enumerate(OWN[:-1]):
            slot = jnp.where(m == place, value, slot)
        return slot

    own_len = len_ref[2 * y + own_i]
    lane = lax.broadcasted_iota(jnp.int32, (1, 128), 1)
    for t in range(4):
        first = own_len - (span - 1) + 16 * (2 * source_of(z, t) + core)
        lim[0, :, pl.ds(128 * t, 128)] = first + lane // 8

    def split_queries(part):
        @pl.loop(0, HALF // 128)
        def _(n):
            q = qb[pl.ds(64 * part + 16 * n, 16)].reshape(128, 128) * scale
            q6[part, pl.ds(pl.multiple_of(128 * n, 128), 128), :] = query_terms(q)

    def prefill_queries():
        for t in range(4):
            part = qb.at[pl.ds(16 * t, 16)]
            pltpu.make_async_copy(part, part, sem_pq_r.at[t]).wait()
        split_queries(0)
        m_ref[0] = jnp.full((1, HALF), NEG_FILL, F32)
        l_ref[0] = jnp.zeros((1, HALF), F32)
        acc[0] = jnp.zeros((128, HALF), F32)

    def decode_queries():
        @pl.loop(0, 16)
        def _(s):
            part = qb.at[pl.ds(64 + 4 * s, 4)]
            pltpu.make_async_copy(part, part, sem_dq_r.at[s, 0]).wait()
            pltpu.make_async_copy(db.at[s], db.at[s], sem_dq_r.at[s, 1]).wait()
            pltpu.make_async_copy(lb.at[s], lb.at[s], sem_dq_r.at[s, 2]).wait()

        for v in range(4):
            row = jnp.where(
                lane < 64,
                jnp.where(lane < 32, lb[4 * v], lb[4 * v + 1]),
                jnp.where(lane < 96, lb[4 * v + 2], lb[4 * v + 3]),
            )
            lim[1, :, pl.ds(128 * v, 128)] = row
        split_queries(1)
        drafts = db[...].reshape(64, 2, 128)
        s = dot_nt(key_terms(drafts[:, 0]), q6[1])
        key_id = lax.broadcasted_iota(jnp.int32, (64, HALF), 0)
        query_id = lax.broadcasted_iota(jnp.int32, (64, HALF), 1) // 8
        s = jnp.where((key_id // 4 == query_id // 4) & (key_id <= query_id), s, NEG_FILL)
        top = jnp.max(s, axis=0, keepdims=True)
        p = jnp.exp2(s - top)
        m_ref[1] = top
        l_ref[1] = jnp.sum(p, axis=0, keepdims=True)
        acc[1] = weighted(value_terms(drafts[:, 1]), p)

    def ready(m):
        u = own_slot(m)
        crossed(u + 8)
        for k in range(2):
            owner = core if k == 0 else 1 - core
            k6[m, owner] = key_terms(kvb[u + 8 * k, 0])
            v2b[m, owner] = value_terms(kvb[u + 8 * k, 1])

    def attend(m, part):
        u = own_slot(m)
        first = 2 * BLK * source_of(jnp.where(u < 4, z, mate), u % 4)
        s = dot_nt(k6[m].reshape(2 * BLK, 768), q6[part])
        place = lax.broadcasted_iota(jnp.int32, (2 * BLK, HALF), 0)
        s = jnp.where(place < lim[part] - first, s, NEG_FILL)
        old = m_ref[part]
        top = jnp.maximum(old, jnp.max(s, axis=0, keepdims=True))
        fade = jnp.exp2(old - top)
        p = jnp.exp2(s - top)
        m_ref[part] = top
        l_ref[part] = l_ref[part] * fade + jnp.sum(p, axis=0, keepdims=True)
        values = jnp.concatenate([v2b[m, 0], v2b[m, 1]], axis=1)
        acc[part] = acc[part] * fade + weighted(values, p)

    for what, which in PLAN:
        if what == "hear":
            hear(which)
        elif what == "tell":
            tell(which)
        elif what == "y":
            along_y()
        elif what == "relay":
            along_y_done()
        elif what == "prefill":
            pq_copy(which).start()
        elif what == "decode":
            for g in range(4):
                dq_start(which, g)
        elif what == "keys":
            kv_primary(*which).start()
        elif what == "keep":
            for h in range(PIECES):
                src, dst = sendb.at[pair, :, piece(h)], kvb.at[0, :, piece(h)]
                pltpu.make_async_copy(src, dst, sem_k_r.at[0, h]).start()
        elif what == "arrive":
            arrive(jnp.int32(OWN[which[0]]), which[1])
        elif what == "prefill queries":
            prefill_queries()
        elif what == "decode queries":
            decode_queries()
        elif what == "ready":
            ready(which)
        elif what == "attend":
            attend(*which)

    def send_on(m, spot):
        for h in range(PIECES):
            if SPOT[h] != spot:
                continue
            go = m + 1 < 8
            for name, place in PLAN:
                if name == "arrive" and place[1] == h and place[0] > EARLY:
                    go = go & (m + 1 != place[0])

            @pl.when(go)
            def _():
                arrive(own_slot(m + 1), h)

    @pl.loop(EARLY, 7)
    def _(m):
        send_on(m, 0)
        ready(m)
        attend(m, 0)
        send_on(m, 1)
        attend(m, 1)
        send_on(m, 2)

    rows_j = pl.ds(pl.multiple_of(8 * own_j, 8), 8)

    def po_copy(t):
        src = ob.at[pl.ds(16 * t, 16)]
        dst = po_ref.at[own_i, :, rows_j, :]
        if t == 0:
            return pltpu.make_async_copy(src, dst, sem_po_r.at[0])
        return pltpu.make_async_remote_copy(
            src,
            dst,
            sem_po_s.at[t],
            sem_po_r.at[t],
            device_id=(2 * source_of(z, t) + core, y, x),
            device_id_type=MESH,
        )

    def do_ends(t, r):
        return ob.at[pl.ds(64 + 16 * t + 4 * r, 4)], do_ref.at[2 * y + own_i, :, rows_j, :]

    def do_remote(t, r):
        src, dst = do_ends(t, r)
        return pltpu.make_async_remote_copy(
            src,
            dst,
            sem_do_s.at[4 * t + r],
            sem_do_r.at[4 * t + y],
            device_id=(2 * source_of(z, t) + core, x, r),
            device_id_type=MESH,
        )

    def do_start(t, r):
        if t:
            do_remote(t, r).start()
            return
        mine = (x == r) & diag

        @pl.when(mine)
        def _():
            src, dst = do_ends(t, r)
            pltpu.make_async_copy(src, dst, sem_do_r.at[4 * t + y]).start()

        @pl.when(jnp.logical_not(mine))
        def _():
            do_remote(t, r).start()

    ready(7)
    for qc in (3, 2, 1, 0):
        if qc % 2:
            attend(7, qc // 2)
        cols = pl.ds(256 * (qc % 2), 256)
        out = acc[qc // 2, :, cols] * (1.0 / l_ref[qc // 2, :, cols])
        ob[pl.ds(32 * qc, 32)] = out.T.reshape(32, 8, 128)
        for t in (2 * (qc % 2) + 1, 2 * (qc % 2)):
            if qc < 2:
                po_copy(t).start()
            else:
                for r in range(4):
                    do_start(t, r)

    for g in range(4):

        @pl.when(y != g)
        def _():
            for copy in y_copies(g):
                copy.wait_send()

    for t in range(1, 4):
        pq_copy(t).wait_send()
    for t in range(4):
        for g in range(4):
            dq_wait_send(t, g)
        for h in range(PIECES):
            if t:
                kv_primary(t, h).wait_send()
            kv_forward(t, h).wait_send()
    for u in range(8):
        for h in range(PIECES):
            kv_cross(u, h).wait_send()
    for t in range(4):
        if t:
            po_copy(t).wait_send()
        p = dest(t) // 2
        rows = pl.ds(pl.multiple_of(8 * (p % 2), 8), 8)
        got = po_ref.at[p // 2, :, rows, :]
        pltpu.make_async_copy(got, got, sem_po_r.at[t]).wait()
        for g in range(4):
            if t:
                do_remote(t, g).wait_send()
            else:

                @pl.when(jnp.logical_not((x == g) & diag))
                def _():
                    do_remote(t, g).wait_send()

            got = do_ref.at[2 * g + p // 2, :, rows, :]
            pltpu.make_async_copy(got, got, sem_do_r.at[4 * t + g]).wait()


def hand_over(here, also_here, there, also_there, held, also_held, sem_in, sem_out):
    ends = ((here, held, there), (also_here, also_held, also_there))
    for n, (src, mid, dst) in enumerate(ends):
        pltpu.make_async_copy(src, mid, sem_in.at[n]).start()
    for n, (src, mid, dst) in enumerate(ends):
        pltpu.make_async_copy(src, mid, sem_in.at[n]).wait()
        pltpu.make_async_copy(mid, dst, sem_out.at[n]).start()
    for n, (src, mid, dst) in enumerate(ends):
        pltpu.make_async_copy(mid, dst, sem_out.at[n]).wait()


def on_device(kv_cache, prefill_q, decode_q, decode_kv, lengths, row_length):
    head_dim = prefill_q.shape[-1]
    span = prefill_q.shape[1] * lax.axis_size("ctx")
    scale = math.log2(math.e) / math.sqrt(head_dim)
    hbm = pl.BlockSpec(memory_space=pltpu.MemorySpace.HBM)
    dma = pltpu.SemaphoreType.DMA
    prefill_out, decode_out = pl.pallas_call(
        functools.partial(kernel, scale, span),
        out_shape=(
            jax.ShapeDtypeStruct((2, 16, 16, 128), F32),
            jax.ShapeDtypeStruct((8, 4, 16, 128), F32),
        ),
        in_specs=[pl.BlockSpec(memory_space=pltpu.SMEM)] * 2 + [hbm] * 4,
        out_specs=(hbm, hbm),
        scratch_shapes=[
            pltpu.VMEM((2, 2, 512, 128), F32),
            pltpu.VMEM((4, 2, BLK, 128), F32),
            pltpu.VMEM((16, 2, BLK, 128), F32),
            pltpu.VMEM((128, 128), F32),
            pltpu.VMEM((8, 2, 8, 128), F32),
            pltpu.VMEM((8, 1, 128), jnp.int32),
            pltpu.VMEM((4, 2, 4, 16, 128), F32),
            pltpu.VMEM((4, 2, 2, 8, 128), F32),
            pltpu.VMEM((4, 2, 1, 128), jnp.int32),
            pltpu.VMEM((128, 8, 128), F32),
            pltpu.VMEM((16, 1, 128), jnp.int32),
            pltpu.VMEM((16, 8, 128), F32),
            pltpu.VMEM((2, HALF, 768), BF16),
            pltpu.VMEM((8, 2, BLK, 768), BF16),
            pltpu.VMEM((8, 2, 256, BLK), BF16),
            pltpu.VMEM((2, 1, HALF), jnp.int32),
            pltpu.VMEM((2, 1, HALF), F32),
            pltpu.VMEM((2, 1, HALF), F32),
            pltpu.VMEM((2, 128, HALF), F32),
            pltpu.VMEM((128, 8, 128), F32),
            dma((2,)),
            pltpu.SemaphoreType.REGULAR((3,)),
            dma((4, 3)),
            dma((4, 3)),
            dma((4,)),
            dma((4,)),
            dma((16, 3)),
            dma((16, 3)),
            dma((4, PIECES)),
            dma((4, PIECES)),
            dma((8, PIECES)),
            dma((16, PIECES)),
            dma((4,)),
            dma((4,)),
            dma((16,)),
            dma((16,)),
        ],
        compiler_params=pltpu.CompilerParams(
            collective_id=0, has_side_effects=True, vmem_limit_bytes=56 * 1024 * 1024
        ),
    )(
        lengths,
        row_length.reshape(8),
        kv_cache.reshape(2, 2, 512, 128),
        prefill_q,
        decode_q.reshape(8, 4, 16, 128),
        decode_kv.reshape(128, 128),
    )
    shapes = [prefill_out.shape, decode_out.shape]
    prefill_out, decode_out = pl.pallas_call(
        hand_over,
        out_shape=[jax.ShapeDtypeStruct(shape, F32) for shape in shapes],
        in_specs=[hbm] * 2,
        out_specs=[hbm] * 2,
        scratch_shapes=[pltpu.VMEM(shape, F32) for shape in shapes] + [dma((2,)), dma((2,))],
    )(prefill_out, decode_out)
    return prefill_out, decode_out.reshape(decode_q.shape)


def solution(mesh):
    in_specs = (
        P("head", None, "ctx", "rep", None),
        P("head", "ctx", "rep", None),
        P(None, ("ctx", "rep"), None, "head", None),
        P(None, ("ctx", "rep"), None, None, "head", None),
        P(),
        P(None, ("ctx", "rep")),
    )
    out_specs = (P("head", "ctx", "rep", None), P(None, ("ctx", "rep"), None, "head", None))
    return jax.shard_map(
        on_device, mesh=mesh, in_specs=in_specs, out_specs=out_specs, check_vma=False
    )
```

```python
import functools
import math

import jax
import jax.numpy as jnp
from jax import lax
from jax.experimental import pallas as pl
from jax.experimental.pallas import tpu as pltpu
from jax.sharding import PartitionSpec as P

MESH = pl.DeviceIdType.MESH
NEG_FILL = -1e30
F32 = jnp.float32
BF16 = jnp.bfloat16
CHIPS = 8
HALF = 512
BLK = 256
PIECES = 2
PIECE = BLK // PIECES
OWN = (0, 4, 1, 5, 3, 2, 7, 6)
SPOT = (1, 1)
PLAN = (
    ("y", 0),
    ("keep", 0),
    ("prefill", 1),
    ("prefill", 0),
    ("arrive", (0, 0)),
    ("hear", 0),
    ("tell", 1),
    ("prefill", 2),
    ("arrive", (0, 1)),
    ("hear", 1),
    ("tell", 2),
    ("prefill", 3),
    ("keys", (1, 0)),
    ("keys", (1, 1)),
    ("keys", (2, 0)),
    ("relay", 0),
    ("hear", 2),
    ("decode", 3),
    ("decode", 1),
    ("decode", 2),
    ("decode", 0),
    ("keys", (3, 0)),
    ("keys", (2, 1)),
    ("keys", (3, 1)),
    ("prefill queries", 0),
    ("ready", 0),
    ("attend", (0, 0)),
    ("arrive", (1, 0)),
    ("arrive", (1, 1)),
    ("ready", 1),
    ("attend", (1, 0)),
    ("arrive", (2, 0)),
    ("arrive", (2, 1)),
    ("ready", 2),
    ("attend", (2, 0)),
    ("arrive", (5, 0)),
    ("decode queries", 0),
    ("attend", (0, 1)),
    ("attend", (1, 1)),
    ("arrive", (3, 0)),
    ("arrive", (3, 1)),
    ("attend", (2, 1)),
    ("arrive", (4, 0)),
)
EARLY = 1 + max(which for what, which in PLAN if what == "ready")


def split2(x):
    hi = x.astype(BF16)
    return hi, (x - hi.astype(F32)).astype(BF16)


def split3(x):
    hi = x.astype(BF16)
    rest = x - hi.astype(F32)
    mid = rest.astype(BF16)
    return hi, mid, (rest - mid.astype(F32)).astype(BF16)


def key_terms(k):
    hi, mid, lo = split3(k)
    return jnp.concatenate([hi, hi, mid, mid, hi, lo], axis=1)


def query_terms(q):
    hi, mid, lo = split3(q)
    return jnp.concatenate([hi, mid, hi, mid, lo, hi], axis=1)


def value_terms(v):
    hi, lo = split2(v.T)
    return jnp.concatenate([hi, lo], axis=0)


def dot_nt(a, b):
    return lax.dot_general(a, b, (((1,), (1,)), ((), ())), preferred_element_type=F32)


def weighted(v2, p):
    hi, lo = split2(p)
    both = jnp.dot(v2, hi, preferred_element_type=F32) + jnp.dot(v2, lo, preferred_element_type=F32)
    return both[:128] + both[128:]


def kernel(
    scale,
    span,
    len_ref,
    rl_ref,
    kv_ref,
    pq_ref,
    dq_ref,
    dkv_ref,
    po_ref,
    do_ref,
    raw,
    sendb,
    kvb,
    dkv,
    dsend,
    rlb,
    rq,
    rd,
    rr,
    qb,
    lb,
    db,
    q6,
    k6,
    v2b,
    lim,
    m_ref,
    l_ref,
    acc,
    ob,
    sem_local,
    near,
    sem_y_s,
    sem_y_r,
    sem_pq_s,
    sem_pq_r,
    sem_dq_s,
    sem_dq_r,
    sem_kp_s,
    sem_kf_s,
    sem_kx_s,
    sem_k_r,
    sem_po_s,
    sem_po_r,
    sem_do_s,
    sem_do_r,
):
    c = lax.axis_index("ctx")
    y = lax.axis_index("head")
    x = lax.axis_index("rep")
    z = c // 2
    core = c % 2

    def dest(t):
        even = (z + t) % 2 == 0
        return lax.rem(jnp.where(even, z + t, z - t + CHIPS), CHIPS)

    def source_of(chip, t):
        return lax.rem(jnp.where(chip % 2 == 0, chip - t + CHIPS, chip + t), CHIPS)

    mate = z + 1 - 2 * (z % 2)
    pair = z // 2
    own_i = pair // 2
    own_j = pair % 2
    diag = x == y

    load = pltpu.make_async_copy(kv_ref, raw, sem_local.at[0])
    load.start()
    load_d = pltpu.make_async_copy(dkv_ref, dkv, sem_local.at[1])
    load_d.start()

    barrier = pltpu.get_barrier_semaphore()

    def greet(ctx, head, rep):
        pl.semaphore_signal(barrier, inc=1, device_id=(ctx, head, rep), device_id_type=MESH)

    up = 2 * lax.rem(z + 1, CHIPS) + core
    down = 2 * lax.rem(z + CHIPS - 1, CHIPS) + core
    greet(2 * z + 1 - core, y, x)
    greet(up, y, x)
    greet(down, y, x)
    for step in range(1, 4):
        greet(c, lax.rem(y + step, 4), x)
        greet(c, y, lax.rem(x + step, 4))

    for req in range(8):
        rlb[req] = jnp.full((1, 128), rl_ref[req], jnp.int32)
    load_d.wait()
    for j in range(2):
        dsend[:, j] = dkv[pl.ds(j, 64, stride=2), :].reshape(8, 8, 128)
    load.wait()
    for i in range(2):
        for s in range(2):
            for j in range(2):
                sendb[2 * i + j, s] = raw[i, s, pl.ds(j, BLK, stride=2), :]

    pl.semaphore_wait(barrier, 9)

    def tell(n):
        for there in (up, down):
            pl.semaphore_signal(near.at[n], inc=1, device_id=(there, y, x), device_id_type=MESH)

    def hear(n):
        pl.semaphore_wait(near.at[n], 2)

    tell(0)

    def y_copies(g):
        reqs = pl.ds(2 * g, 2)
        return [
            pltpu.make_async_remote_copy(
                src,
                dst,
                sem_y_s.at[n],
                sem_y_r.at[n],
                device_id=(c, g, x),
                device_id_type=MESH,
            )
            for n, (src, dst) in enumerate(
                ((dq_ref.at[reqs], rq.at[y]), (dsend.at[reqs], rd.at[y]), (rlb.at[reqs], rr.at[y]))
            )
        ]

    def y_keep():
        reqs = pl.ds(pl.multiple_of(2 * y, 2), 2)
        return [
            pltpu.make_async_copy(src, dst, sem_y_r.at[n])
            for n, (src, dst) in enumerate(
                ((dq_ref.at[reqs], rq.at[y]), (dsend.at[reqs], rd.at[y]), (rlb.at[reqs], rr.at[y]))
            )
        ]

    def pq_copy(t):
        zt = dest(t)
        p = zt // 2
        src = pq_ref.at[p // 2, :, pl.ds(pl.multiple_of(8 * (p % 2), 8), 8), :]
        dst = qb.at[pl.ds(16 * t, 16)]
        if t == 0:
            return pltpu.make_async_copy(src, dst, sem_pq_r.at[0])
        return pltpu.make_async_remote_copy(
            src, dst, sem_pq_s.at[0], sem_pq_r.at[0], device_id=(2 * zt + core, y, x), device_id_type=MESH
        )

    def dq_parts(t, h):
        p = dest(t) // 2
        i, j = p // 2, p % 2
        slot = 4 * t + x
        return (
            (rq.at[h, i, :, pl.ds(pl.multiple_of(8 * j, 8), 8), :], qb.at[pl.ds(64 + 4 * slot, 4)]),
            (rd.at[h, i, j], db.at[slot]),
            (rr.at[h, i], lb.at[slot]),
        )

    def dq_remote(t, h, n, part):
        return pltpu.make_async_remote_copy(
            part[0],
            part[1],
            sem_dq_s.at[n],
            sem_dq_r.at[n],
            device_id=(2 * dest(t) + core, y, h),
            device_id_type=MESH,
        )

    def dq_start(t, h):
        for n, part in enumerate(dq_parts(t, h)):
            if t:
                dq_remote(t, h, n, part).start()
            else:

                @pl.when(x == h)
                def _():
                    pltpu.make_async_copy(part[0], part[1], sem_dq_r.at[n]).start()

                @pl.when(x != h)
                def _():
                    dq_remote(t, h, n, part).start()

    def piece(h):
        return pl.ds(PIECE * h, PIECE)

    def kv_primary(t, h):
        zt = dest(t)
        return pltpu.make_async_remote_copy(
            sendb.at[zt // 2, :, piece(h)],
            kvb.at[t, :, piece(h)],
            sem_kp_s.at[t],
            sem_k_r.at[t, h],
            device_id=(2 * zt + core, y, x),
            device_id_type=MESH,
        )

    def kv_forward(t, h):
        return pltpu.make_async_remote_copy(
            kvb.at[t, :, piece(h)],
            kvb.at[t + 4, :, piece(h)],
            sem_kf_s.at[t],
            sem_k_r.at[t + 4, h],
            device_id=(2 * mate + core, y, x),
            device_id_type=MESH,
        )

    def kv_cross(u, h):
        return pltpu.make_async_remote_copy(
            kvb.at[u, :, piece(h)],
            kvb.at[u + 8, :, piece(h)],
            sem_kx_s.at[u],
            sem_k_r.at[u + 8, h],
            device_id=(2 * z + 1 - core, y, x),
            device_id_type=MESH,
        )

    def arrive(u, h):
        part = kvb.at[u, :, piece(h)]
        pltpu.make_async_copy(part, part, sem_k_r.at[u, h]).wait()

        @pl.when(u < 4)
        def _():
            kv_forward(u, h).start()

        kv_cross(u, h).start()

    def crossed(u):
        for h in range(PIECES):
            part = kvb.at[u, :, piece(h)]
            pltpu.make_async_copy(part, part, sem_k_r.at[u, h]).wait()

    def along_y():
        for g in range(4):

            @pl.when(y == g)
            def _():
                for copy in y_keep():
                    copy.start()

            @pl.when(y != g)
            def _():
                for copy in y_copies(g):
                    copy.start()

    def along_y_done():
        for n, part in enumerate((rq, rd, rr)):
            pltpu.make_async_copy(part, part, sem_y_r.at[n]).wait()

    def own_slot(m):
        slot = OWN[-1]
        for place, value in enumerate(OWN[:-1]):
            slot = jnp.where(m == place, value, slot)
        return slot

    own_len = len_ref[2 * y + own_i]
    lane = lax.broadcasted_iota(jnp.int32, (1, 128), 1)
    for t in range(4):
        first = own_len - (span - 1) + 16 * (2 * source_of(z, t) + core)
        lim[0, :, pl.ds(128 * t, 128)] = first + lane // 8

    def split_queries(part):
        @pl.loop(0, HALF // 128)
        def _(n):
            q = qb[pl.ds(64 * part + 16 * n, 16)].reshape(128, 128) * scale
            q6[part, pl.ds(pl.multiple_of(128 * n, 128), 128), :] = query_terms(q)

    def prefill_queries():
        part = qb.at[pl.ds(0, 64)]
        pltpu.make_async_copy(part, part, sem_pq_r.at[0]).wait()
        split_queries(0)
        m_ref[0] = jnp.full((1, HALF), NEG_FILL, F32)
        l_ref[0] = jnp.zeros((1, HALF), F32)
        acc[0] = jnp.zeros((128, HALF), F32)

    def decode_queries():
        for n, part in enumerate((qb.at[pl.ds(64, 64)], db, lb)):
            pltpu.make_async_copy(part, part, sem_dq_r.at[n]).wait()

        for v in range(4):
            row = jnp.where(
                lane < 64,
                jnp.where(lane < 32, lb[4 * v], lb[4 * v + 1]),
                jnp.where(lane < 96, lb[4 * v + 2], lb[4 * v + 3]),
            )
            lim[1, :, pl.ds(128 * v, 128)] = row
        split_queries(1)
        drafts = db[...].reshape(64, 2, 128)
        s = dot_nt(key_terms(drafts[:, 0]), q6[1])
        key_id = lax.broadcasted_iota(jnp.int32, (64, HALF), 0)
        query_id = lax.broadcasted_iota(jnp.int32, (64, HALF), 1) // 8
        s = jnp.where((key_id // 4 == query_id // 4) & (key_id <= query_id), s, NEG_FILL)
        top = jnp.max(s, axis=0, keepdims=True)
        p = jnp.exp2(s - top)
        m_ref[1] = top
        l_ref[1] = jnp.sum(p, axis=0, keepdims=True)
        acc[1] = weighted(value_terms(drafts[:, 1]), p)

    def ready(m):
        u = own_slot(m)
        crossed(u + 8)
        for k in range(2):
            owner = core if k == 0 else 1 - core
            k6[m, owner] = key_terms(kvb[u + 8 * k, 0])
            v2b[m, owner] = value_terms(kvb[u + 8 * k, 1])

    def attend(m, part):
        u = own_slot(m)
        first = 2 * BLK * source_of(jnp.where(u < 4, z, mate), u % 4)
        s = dot_nt(k6[m].reshape(2 * BLK, 768), q6[part])
        place = lax.broadcasted_iota(jnp.int32, (2 * BLK, HALF), 0)
        s = jnp.where(place < lim[part] - first, s, NEG_FILL)
        old = m_ref[part]
        top = jnp.maximum(old, jnp.max(s, axis=0, keepdims=True))
        fade = jnp.exp2(old - top)
        p = jnp.exp2(s - top)
        m_ref[part] = top
        l_ref[part] = l_ref[part] * fade + jnp.sum(p, axis=0, keepdims=True)
        values = jnp.concatenate([v2b[m, 0], v2b[m, 1]], axis=1)
        acc[part] = acc[part] * fade + weighted(values, p)

    for what, which in PLAN:
        if what == "hear":
            hear(which)
        elif what == "tell":
            tell(which)
        elif what == "y":
            along_y()
        elif what == "relay":
            along_y_done()
        elif what == "prefill":
            pq_copy(which).start()
        elif what == "decode":
            for g in range(4):
                dq_start(which, g)
        elif what == "keys":
            kv_primary(*which).start()
        elif what == "keep":
            for h in range(PIECES):
                src, dst = sendb.at[pair, :, piece(h)], kvb.at[0, :, piece(h)]
                pltpu.make_async_copy(src, dst, sem_k_r.at[0, h]).start()
        elif what == "arrive":
            arrive(jnp.int32(OWN[which[0]]), which[1])
        elif what == "prefill queries":
            prefill_queries()
        elif what == "decode queries":
            decode_queries()
        elif what == "ready":
            ready(which)
        elif what == "attend":
            attend(*which)

    def send_on(m, spot):
        for h in range(PIECES):
            if SPOT[h] != spot:
                continue
            go = m + 1 < 8
            for name, place in PLAN:
                if name == "arrive" and place[1] == h and place[0] > EARLY:
                    go = go & (m + 1 != place[0])

            @pl.when(go)
            def _():
                arrive(own_slot(m + 1), h)

    @pl.loop(EARLY, 7)
    def _(m):
        send_on(m, 0)
        ready(m)
        attend(m, 1)
        send_on(m, 1)

        @pl.when(m % 2 == 1)
        def _():
            attend((m + 3) // 2, 0)

        send_on(m, 2)

    rows_j = pl.ds(pl.multiple_of(8 * own_j, 8), 8)

    def po_copy(t):
        src = ob.at[pl.ds(16 * t, 16)]
        dst = po_ref.at[own_i, :, rows_j, :]
        if t == 0:
            return pltpu.make_async_copy(src, dst, sem_po_r.at[0])
        return pltpu.make_async_remote_copy(
            src,
            dst,
            sem_po_s.at[0],
            sem_po_r.at[0],
            device_id=(2 * source_of(z, t) + core, y, x),
            device_id_type=MESH,
        )

    def do_ends(t, r):
        return ob.at[pl.ds(64 + 16 * t + 4 * r, 4)], do_ref.at[2 * y + own_i, :, rows_j, :]

    def do_remote(t, r):
        src, dst = do_ends(t, r)
        return pltpu.make_async_remote_copy(
            src,
            dst,
            sem_do_s.at[4 if t else r],
            sem_do_r.at[0],
            device_id=(2 * source_of(z, t) + core, x, r),
            device_id_type=MESH,
        )

    def do_start(t, r):
        if t:
            do_remote(t, r).start()
            return
        mine = (x == r) & diag

        @pl.when(mine)
        def _():
            src, dst = do_ends(t, r)
            pltpu.make_async_copy(src, dst, sem_do_r.at[0]).start()

        @pl.when(jnp.logical_not(mine))
        def _():
            do_remote(t, r).start()

    ready(7)
    for qc in (3, 2, 1, 0):
        if qc == 3:
            attend(7, 1)
        elif qc == 1:

            @pl.loop(5, 8)
            def _(m):
                attend(m, 0)

        cols = pl.ds(256 * (qc % 2), 256)
        out = acc[qc // 2, :, cols] * (1.0 / l_ref[qc // 2, :, cols])
        ob[pl.ds(32 * qc, 32)] = out.T.reshape(32, 8, 128)
        for t in (2 * (qc % 2) + 1, 2 * (qc % 2)):
            if qc < 2:
                po_copy(t).start()
            else:
                for r in range(4):
                    do_start(t, r)

    def ended(part, sem):
        pltpu.make_async_copy(part, part, sem).wait()

    for n, part in enumerate((rq, rd, rr)):
        ended(part.at[pl.ds(0, 3)], sem_y_s.at[n])
    ended(qb.at[pl.ds(0, 48)], sem_pq_s.at[0])
    for n, part in enumerate((qb.at[pl.ds(0, 60)], db.at[pl.ds(0, 15)], lb.at[pl.ds(0, 15)])):
        ended(part, sem_dq_s.at[n])
    for t in range(4):
        if t:
            ended(kvb.at[t], sem_kp_s.at[t])
        ended(kvb.at[t], sem_kf_s.at[t])
    for u in range(8):
        ended(kvb.at[u], sem_kx_s.at[u])
    ended(ob.at[pl.ds(0, 48)], sem_po_s.at[0])
    for r in range(4):

        @pl.when(jnp.logical_not((x == r) & diag))
        def _():
            do_remote(0, r).wait_send()

    ended(ob.at[pl.ds(80, 48)], sem_do_s.at[4])
    ended(po_ref, sem_po_r.at[0])
    ended(do_ref, sem_do_r.at[0])


def hand_over(here, also_here, there, also_there, held, also_held, sem_in, sem_out):
    ends = ((here, held, there), (also_here, also_held, also_there))
    for n, (src, mid, dst) in enumerate(ends):
        pltpu.make_async_copy(src, mid, sem_in.at[n]).start()
    for n, (src, mid, dst) in enumerate(ends):
        pltpu.make_async_copy(src, mid, sem_in.at[n]).wait()
        pltpu.make_async_copy(mid, dst, sem_out.at[n]).start()
    for n, (src, mid, dst) in enumerate(ends):
        pltpu.make_async_copy(mid, dst, sem_out.at[n]).wait()


def on_device(kv_cache, prefill_q, decode_q, decode_kv, lengths, row_length):
    head_dim = prefill_q.shape[-1]
    span = prefill_q.shape[1] * lax.axis_size("ctx")
    scale = math.log2(math.e) / math.sqrt(head_dim)
    hbm = pl.BlockSpec(memory_space=pltpu.MemorySpace.HBM)
    dma = pltpu.SemaphoreType.DMA
    prefill_out, decode_out = pl.pallas_call(
        functools.partial(kernel, scale, span),
        out_shape=(
            jax.ShapeDtypeStruct((2, 16, 16, 128), F32),
            jax.ShapeDtypeStruct((8, 4, 16, 128), F32),
        ),
        in_specs=[pl.BlockSpec(memory_space=pltpu.SMEM)] * 2 + [hbm] * 4,
        out_specs=(hbm, hbm),
        scratch_shapes=[
            pltpu.VMEM((2, 2, 512, 128), F32),
            pltpu.VMEM((4, 2, BLK, 128), F32),
            pltpu.VMEM((16, 2, BLK, 128), F32),
            pltpu.VMEM((128, 128), F32),
            pltpu.VMEM((8, 2, 8, 128), F32),
            pltpu.VMEM((8, 1, 128), jnp.int32),
            pltpu.VMEM((4, 2, 4, 16, 128), F32),
            pltpu.VMEM((4, 2, 2, 8, 128), F32),
            pltpu.VMEM((4, 2, 1, 128), jnp.int32),
            pltpu.VMEM((128, 8, 128), F32),
            pltpu.VMEM((16, 1, 128), jnp.int32),
            pltpu.VMEM((16, 8, 128), F32),
            pltpu.VMEM((2, HALF, 768), BF16),
            pltpu.VMEM((8, 2, BLK, 768), BF16),
            pltpu.VMEM((8, 2, 256, BLK), BF16),
            pltpu.VMEM((2, 1, HALF), jnp.int32),
            pltpu.VMEM((2, 1, HALF), F32),
            pltpu.VMEM((2, 1, HALF), F32),
            pltpu.VMEM((2, 128, HALF), F32),
            pltpu.VMEM((128, 8, 128), F32),
            dma((2,)),
            pltpu.SemaphoreType.REGULAR((3,)),
            dma((3,)),
            dma((3,)),
            dma((1,)),
            dma((1,)),
            dma((3,)),
            dma((3,)),
            dma((4,)),
            dma((4,)),
            dma((8,)),
            dma((16, PIECES)),
            dma((1,)),
            dma((1,)),
            dma((5,)),
            dma((1,)),
        ],
        compiler_params=pltpu.CompilerParams(
            collective_id=0, has_side_effects=True, vmem_limit_bytes=56 * 1024 * 1024
        ),
    )(
        lengths,
        row_length.reshape(8),
        kv_cache.reshape(2, 2, 512, 128),
        prefill_q,
        decode_q.reshape(8, 4, 16, 128),
        decode_kv.reshape(128, 128),
    )
    shapes = [prefill_out.shape, decode_out.shape]
    prefill_out, decode_out = pl.pallas_call(
        hand_over,
        out_shape=[jax.ShapeDtypeStruct(shape, F32) for shape in shapes],
        in_specs=[hbm] * 2,
        out_specs=[hbm] * 2,
        scratch_shapes=[pltpu.VMEM(shape, F32) for shape in shapes] + [dma((2,)), dma((2,))],
    )(prefill_out, decode_out)
    return prefill_out, decode_out.reshape(decode_q.shape)


def solution(mesh):
    in_specs = (
        P("head", None, "ctx", "rep", None),
        P("head", "ctx", "rep", None),
        P(None, ("ctx", "rep"), None, "head", None),
        P(None, ("ctx", "rep"), None, None, "head", None),
        P(),
        P(None, ("ctx", "rep")),
    )
    out_specs = (P("head", "ctx", "rep", None), P(None, ("ctx", "rep"), None, "head", None))
    return jax.shard_map(
        on_device, mesh=mesh, in_specs=in_specs, out_specs=out_specs, check_vma=False
    )
```

```python
import functools
import math

import jax
import jax.numpy as jnp
from jax import lax
from jax.experimental import pallas as pl
from jax.experimental.pallas import tpu as pltpu
from jax.sharding import PartitionSpec as P

MESH = pl.DeviceIdType.MESH
NEG_FILL = -1e30
F32 = jnp.float32
BF16 = jnp.bfloat16
CHIPS = 8
HALF = 512
BLK = 256
PIECES = 2
PIECE = BLK // PIECES
OWN = (0, 4, 1, 5, 2, 3, 6, 7)
SPOT = (1, 1)
PLAN = (
    ("y", 0),
    ("keep", 0),
    ("prefill", 1),
    ("prefill", 0),
    ("arrive", (0, 0)),
    ("hear", 0),
    ("tell", 1),
    ("prefill", 2),
    ("arrive", (0, 1)),
    ("hear", 1),
    ("tell", 2),
    ("prefill", 3),
    ("keys", (1, 0)),
    ("keys", (1, 1)),
    ("keys", (2, 0)),
    ("relay", 0),
    ("hear", 2),
    ("decode", 3),
    ("decode", 1),
    ("decode", 2),
    ("decode", 0),
    ("keys", (3, 0)),
    ("keys", (2, 1)),
    ("keys", (3, 1)),
    ("prefill queries", 0),
    ("ready", 0),
    ("attend", (0, 0)),
    ("arrive", (1, 0)),
    ("arrive", (1, 1)),
    ("ready", 1),
    ("attend", (1, 0)),
    ("arrive", (2, 0)),
    ("arrive", (2, 1)),
    ("ready", 2),
    ("attend", (2, 0)),
    ("arrive", (4, 0)),
    ("decode queries", 0),
    ("attend", (0, 1)),
    ("attend", (1, 1)),
    ("arrive", (3, 0)),
    ("arrive", (3, 1)),
    ("attend", (2, 1)),
    ("arrive", (5, 0)),
)
EARLY = 1 + max(which for what, which in PLAN if what == "ready")


def split2(x):
    hi = x.astype(BF16)
    return hi, (x - hi.astype(F32)).astype(BF16)


def split3(x):
    hi = x.astype(BF16)
    rest = x - hi.astype(F32)
    mid = rest.astype(BF16)
    return hi, mid, (rest - mid.astype(F32)).astype(BF16)


def key_terms(k):
    hi, mid, lo = split3(k)
    return jnp.concatenate([hi, hi, mid, mid, hi, lo], axis=1)


def query_terms(q):
    hi, mid, lo = split3(q)
    return jnp.concatenate([hi, mid, hi, mid, lo, hi], axis=1)


def value_terms(v):
    hi, lo = split2(v.T)
    return jnp.concatenate([hi, lo], axis=0)


def dot_nt(a, b):
    return lax.dot_general(a, b, (((1,), (1,)), ((), ())), preferred_element_type=F32)


def weighted(v2, p):
    hi, lo = split2(p)
    both = jnp.dot(v2, hi, preferred_element_type=F32) + jnp.dot(v2, lo, preferred_element_type=F32)
    return both[:128] + both[128:]


def kernel(
    scale,
    span,
    len_ref,
    rl_ref,
    kv_ref,
    pq_ref,
    dq_ref,
    dkv_ref,
    po_ref,
    do_ref,
    raw,
    sendb,
    kvb,
    dkv,
    dsend,
    rlb,
    rq,
    rd,
    rr,
    qb,
    lb,
    db,
    q6,
    k6,
    v2b,
    lim,
    m_ref,
    l_ref,
    acc,
    ob,
    sem_local,
    near,
    sem_y_s,
    sem_y_r,
    sem_pq_s,
    sem_pq_r,
    sem_dq_s,
    sem_dq_r,
    sem_kp_s,
    sem_kf_s,
    sem_kx_s,
    sem_k_r,
    sem_po_s,
    sem_po_r,
    sem_do_s,
    sem_do_r,
):
    c = lax.axis_index("ctx")
    y = lax.axis_index("head")
    x = lax.axis_index("rep")
    z = c // 2
    core = c % 2

    def dest(t):
        even = (z + t) % 2 == 0
        return lax.rem(jnp.where(even, z + t, z - t + CHIPS), CHIPS)

    def source_of(chip, t):
        return lax.rem(jnp.where(chip % 2 == 0, chip - t + CHIPS, chip + t), CHIPS)

    mate = z + 1 - 2 * (z % 2)
    pair = z // 2
    own_i = pair // 2
    own_j = pair % 2
    diag = x == y

    load = pltpu.make_async_copy(kv_ref, raw, sem_local.at[0])
    load.start()
    load_d = pltpu.make_async_copy(dkv_ref, dkv, sem_local.at[1])
    load_d.start()

    barrier = pltpu.get_barrier_semaphore()

    def greet(ctx, head, rep):
        pl.semaphore_signal(barrier, inc=1, device_id=(ctx, head, rep), device_id_type=MESH)

    up = 2 * lax.rem(z + 1, CHIPS) + core
    down = 2 * lax.rem(z + CHIPS - 1, CHIPS) + core
    greet(2 * z + 1 - core, y, x)
    greet(up, y, x)
    greet(down, y, x)
    for step in range(1, 4):
        greet(c, lax.rem(y + step, 4), x)
        greet(c, y, lax.rem(x + step, 4))

    for req in range(8):
        rlb[req] = jnp.full((1, 128), rl_ref[req], jnp.int32)
    load_d.wait()
    for j in range(2):
        dsend[:, j] = dkv[pl.ds(j, 64, stride=2), :].reshape(8, 8, 128)
    load.wait()
    for i in range(2):
        for s in range(2):
            for j in range(2):
                sendb[2 * i + j, s] = raw[i, s, pl.ds(j, BLK, stride=2), :]

    pl.semaphore_wait(barrier, 9)

    def tell(n):
        for there in (up, down):
            pl.semaphore_signal(near.at[n], inc=1, device_id=(there, y, x), device_id_type=MESH)

    def hear(n):
        pl.semaphore_wait(near.at[n], 2)

    tell(0)

    def y_copies(g):
        reqs = pl.ds(2 * g, 2)
        return [
            pltpu.make_async_remote_copy(
                src,
                dst,
                sem_y_s.at[n],
                sem_y_r.at[n],
                device_id=(c, g, x),
                device_id_type=MESH,
            )
            for n, (src, dst) in enumerate(
                ((dq_ref.at[reqs], rq.at[y]), (dsend.at[reqs], rd.at[y]), (rlb.at[reqs], rr.at[y]))
            )
        ]

    def y_keep():
        reqs = pl.ds(pl.multiple_of(2 * y, 2), 2)
        return [
            pltpu.make_async_copy(src, dst, sem_y_r.at[n])
            for n, (src, dst) in enumerate(
                ((dq_ref.at[reqs], rq.at[y]), (dsend.at[reqs], rd.at[y]), (rlb.at[reqs], rr.at[y]))
            )
        ]

    def pq_copy(t):
        zt = dest(t)
        p = zt // 2
        src = pq_ref.at[p // 2, :, pl.ds(pl.multiple_of(8 * (p % 2), 8), 8), :]
        dst = qb.at[pl.ds(16 * t, 16)]
        if t == 0:
            return pltpu.make_async_copy(src, dst, sem_pq_r.at[0])
        return pltpu.make_async_remote_copy(
            src, dst, sem_pq_s.at[0], sem_pq_r.at[0], device_id=(2 * zt + core, y, x), device_id_type=MESH
        )

    def dq_parts(t, h):
        p = dest(t) // 2
        i, j = p // 2, p % 2
        slot = 4 * t + x
        return (
            (rq.at[h, i, :, pl.ds(pl.multiple_of(8 * j, 8), 8), :], qb.at[pl.ds(64 + 4 * slot, 4)]),
            (rd.at[h, i, j], db.at[slot]),
            (rr.at[h, i], lb.at[slot]),
        )

    def dq_remote(t, h, n, part):
        return pltpu.make_async_remote_copy(
            part[0],
            part[1],
            sem_dq_s.at[n],
            sem_dq_r.at[n],
            device_id=(2 * dest(t) + core, y, h),
            device_id_type=MESH,
        )

    def dq_start(t, h):
        for n, part in enumerate(dq_parts(t, h)):
            if t:
                dq_remote(t, h, n, part).start()
            else:

                @pl.when(x == h)
                def _():
                    pltpu.make_async_copy(part[0], part[1], sem_dq_r.at[n]).start()

                @pl.when(x != h)
                def _():
                    dq_remote(t, h, n, part).start()

    def piece(h):
        return pl.ds(PIECE * h, PIECE)

    def kv_primary(t, h):
        zt = dest(t)
        return pltpu.make_async_remote_copy(
            sendb.at[zt // 2, :, piece(h)],
            kvb.at[t, :, piece(h)],
            sem_kp_s.at[t],
            sem_k_r.at[t, h],
            device_id=(2 * zt + core, y, x),
            device_id_type=MESH,
        )

    def kv_forward(t, h):
        return pltpu.make_async_remote_copy(
            kvb.at[t, :, piece(h)],
            kvb.at[t + 4, :, piece(h)],
            sem_kf_s.at[t],
            sem_k_r.at[t + 4, h],
            device_id=(2 * mate + core, y, x),
            device_id_type=MESH,
        )

    def kv_cross(u, h):
        return pltpu.make_async_remote_copy(
            kvb.at[u, :, piece(h)],
            kvb.at[u + 8, :, piece(h)],
            sem_kx_s.at[u],
            sem_k_r.at[u + 8, h],
            device_id=(2 * z + 1 - core, y, x),
            device_id_type=MESH,
        )

    def arrive(u, h):
        part = kvb.at[u, :, piece(h)]
        pltpu.make_async_copy(part, part, sem_k_r.at[u, h]).wait()

        @pl.when(u < 4)
        def _():
            kv_forward(u, h).start()

        kv_cross(u, h).start()

    def crossed(u):
        for h in range(PIECES):
            part = kvb.at[u, :, piece(h)]
            pltpu.make_async_copy(part, part, sem_k_r.at[u, h]).wait()

    def along_y():
        for g in range(4):

            @pl.when(y == g)
            def _():
                for copy in y_keep():
                    copy.start()

            @pl.when(y != g)
            def _():
                for copy in y_copies(g):
                    copy.start()

    def along_y_done():
        for n, part in enumerate((rq, rd, rr)):
            pltpu.make_async_copy(part, part, sem_y_r.at[n]).wait()

    def own_slot(m):
        slot = OWN[-1]
        for place, value in enumerate(OWN[:-1]):
            slot = jnp.where(m == place, value, slot)
        return slot

    own_len = len_ref[2 * y + own_i]
    lane = lax.broadcasted_iota(jnp.int32, (1, 128), 1)
    for t in range(4):
        first = own_len - (span - 1) + 16 * (2 * source_of(z, t) + core)
        lim[0, :, pl.ds(128 * t, 128)] = first + lane // 8

    def split_queries(part):
        @pl.loop(0, HALF // 128)
        def _(n):
            q = qb[pl.ds(64 * part + 16 * n, 16)].reshape(128, 128) * scale
            q6[part, pl.ds(pl.multiple_of(128 * n, 128), 128), :] = query_terms(q)

    def prefill_queries():
        part = qb.at[pl.ds(0, 64)]
        pltpu.make_async_copy(part, part, sem_pq_r.at[0]).wait()
        split_queries(0)
        m_ref[0] = jnp.full((1, HALF), NEG_FILL, F32)
        l_ref[0] = jnp.zeros((1, HALF), F32)
        acc[0] = jnp.zeros((128, HALF), F32)

    def decode_queries():
        for n, part in enumerate((qb.at[pl.ds(64, 64)], db, lb)):
            pltpu.make_async_copy(part, part, sem_dq_r.at[n]).wait()

        for v in range(4):
            row = jnp.where(
                lane < 64,
                jnp.where(lane < 32, lb[4 * v], lb[4 * v + 1]),
                jnp.where(lane < 96, lb[4 * v + 2], lb[4 * v + 3]),
            )
            lim[1, :, pl.ds(128 * v, 128)] = row
        split_queries(1)
        drafts = db[...].reshape(64, 2, 128)
        s = dot_nt(key_terms(drafts[:, 0]), q6[1])
        key_id = lax.broadcasted_iota(jnp.int32, (64, HALF), 0)
        query_id = lax.broadcasted_iota(jnp.int32, (64, HALF), 1) // 8
        s = jnp.where((key_id // 4 == query_id // 4) & (key_id <= query_id), s, NEG_FILL)
        top = jnp.max(s, axis=0, keepdims=True)
        p = jnp.exp2(s - top)
        m_ref[1] = top
        l_ref[1] = jnp.sum(p, axis=0, keepdims=True)
        acc[1] = weighted(value_terms(drafts[:, 1]), p)

    def ready(m):
        u = own_slot(m)
        crossed(u + 8)
        for k in range(2):
            owner = core if k == 0 else 1 - core
            k6[m, owner] = key_terms(kvb[u + 8 * k, 0])
            v2b[m, owner] = value_terms(kvb[u + 8 * k, 1])

    def attend(m, part):
        u = own_slot(m)
        first = 2 * BLK * source_of(jnp.where(u < 4, z, mate), u % 4)
        s = dot_nt(k6[m].reshape(2 * BLK, 768), q6[part])
        place = lax.broadcasted_iota(jnp.int32, (2 * BLK, HALF), 0)
        s = jnp.where(place < lim[part] - first, s, NEG_FILL)
        old = m_ref[part]
        top = jnp.maximum(old, jnp.max(s, axis=0, keepdims=True))
        fade = jnp.exp2(old - top)
        p = jnp.exp2(s - top)
        m_ref[part] = top
        l_ref[part] = l_ref[part] * fade + jnp.sum(p, axis=0, keepdims=True)
        values = jnp.concatenate([v2b[m, 0], v2b[m, 1]], axis=1)
        acc[part] = acc[part] * fade + weighted(values, p)

    for what, which in PLAN:
        if what == "hear":
            hear(which)
        elif what == "tell":
            tell(which)
        elif what == "y":
            along_y()
        elif what == "relay":
            along_y_done()
        elif what == "prefill":
            pq_copy(which).start()
        elif what == "decode":
            for g in range(4):
                dq_start(which, g)
        elif what == "keys":
            kv_primary(*which).start()
        elif what == "keep":
            for h in range(PIECES):
                src, dst = sendb.at[pair, :, piece(h)], kvb.at[0, :, piece(h)]
                pltpu.make_async_copy(src, dst, sem_k_r.at[0, h]).start()
        elif what == "arrive":
            arrive(jnp.int32(OWN[which[0]]), which[1])
        elif what == "prefill queries":
            prefill_queries()
        elif what == "decode queries":
            decode_queries()
        elif what == "ready":
            ready(which)
        elif what == "attend":
            attend(*which)

    def send_on(m, spot):
        for h in range(PIECES):
            if SPOT[h] != spot:
                continue
            go = m + 1 < 8
            for name, place in PLAN:
                if name == "arrive" and place[1] == h and place[0] > EARLY:
                    go = go & (m + 1 != place[0])

            @pl.when(go)
            def _():
                arrive(own_slot(m + 1), h)

    @pl.loop(EARLY, 7)
    def _(m):
        send_on(m, 0)
        ready(m)
        attend(m, 1)
        send_on(m, 1)

        @pl.when(m % 2 == 1)
        def _():
            attend((m + 3) // 2, 0)

        send_on(m, 2)

    rows_j = pl.ds(pl.multiple_of(8 * own_j, 8), 8)

    def po_copy(t):
        src = ob.at[pl.ds(16 * t, 16)]
        dst = po_ref.at[own_i, :, rows_j, :]
        if t == 0:
            return pltpu.make_async_copy(src, dst, sem_po_r.at[0])
        return pltpu.make_async_remote_copy(
            src,
            dst,
            sem_po_s.at[0],
            sem_po_r.at[0],
            device_id=(2 * source_of(z, t) + core, y, x),
            device_id_type=MESH,
        )

    def do_ends(t, r):
        return ob.at[pl.ds(64 + 16 * t + 4 * r, 4)], do_ref.at[2 * y + own_i, :, rows_j, :]

    def do_remote(t, r):
        src, dst = do_ends(t, r)
        return pltpu.make_async_remote_copy(
            src,
            dst,
            sem_do_s.at[4 if t else r],
            sem_do_r.at[0],
            device_id=(2 * source_of(z, t) + core, x, r),
            device_id_type=MESH,
        )

    def do_start(t, r):
        if t:
            do_remote(t, r).start()
            return
        mine = (x == r) & diag

        @pl.when(mine)
        def _():
            src, dst = do_ends(t, r)
            pltpu.make_async_copy(src, dst, sem_do_r.at[0]).start()

        @pl.when(jnp.logical_not(mine))
        def _():
            do_remote(t, r).start()

    ready(7)
    for qc in (3, 2, 1, 0):
        if qc == 3:
            attend(7, 1)
        elif qc == 1:

            @pl.loop(5, 8)
            def _(m):
                attend(m, 0)

        cols = pl.ds(256 * (qc % 2), 256)
        out = acc[qc // 2, :, cols] * (1.0 / l_ref[qc // 2, :, cols])
        ob[pl.ds(32 * qc, 32)] = out.T.reshape(32, 8, 128)
        for t in (2 * (qc % 2) + 1, 2 * (qc % 2)):
            if qc < 2:
                po_copy(t).start()
            else:
                for r in range(4):
                    do_start(t, r)

    def ended(part, sem):
        pltpu.make_async_copy(part, part, sem).wait()

    for n, part in enumerate((rq, rd, rr)):
        ended(part.at[pl.ds(0, 3)], sem_y_s.at[n])
    ended(qb.at[pl.ds(0, 48)], sem_pq_s.at[0])
    for n, part in enumerate((qb.at[pl.ds(0, 60)], db.at[pl.ds(0, 15)], lb.at[pl.ds(0, 15)])):
        ended(part, sem_dq_s.at[n])
    for t in range(4):
        if t:
            ended(kvb.at[t], sem_kp_s.at[t])
        ended(kvb.at[t], sem_kf_s.at[t])
    for u in range(8):
        ended(kvb.at[u], sem_kx_s.at[u])
    ended(ob.at[pl.ds(0, 48)], sem_po_s.at[0])
    for r in range(4):

        @pl.when(jnp.logical_not((x == r) & diag))
        def _():
            do_remote(0, r).wait_send()

    ended(ob.at[pl.ds(80, 48)], sem_do_s.at[4])
    ended(po_ref, sem_po_r.at[0])
    ended(do_ref, sem_do_r.at[0])


def hand_over(here, also_here, there, also_there, held, also_held, sem_in, sem_out):
    ends = ((here, held, there), (also_here, also_held, also_there))
    for n, (src, mid, dst) in enumerate(ends):
        pltpu.make_async_copy(src, mid, sem_in.at[n]).start()
    for n, (src, mid, dst) in enumerate(ends):
        pltpu.make_async_copy(src, mid, sem_in.at[n]).wait()
        pltpu.make_async_copy(mid, dst, sem_out.at[n]).start()
    for n, (src, mid, dst) in enumerate(ends):
        pltpu.make_async_copy(mid, dst, sem_out.at[n]).wait()


def on_device(kv_cache, prefill_q, decode_q, decode_kv, lengths, row_length):
    head_dim = prefill_q.shape[-1]
    span = prefill_q.shape[1] * lax.axis_size("ctx")
    scale = math.log2(math.e) / math.sqrt(head_dim)
    hbm = pl.BlockSpec(memory_space=pltpu.MemorySpace.HBM)
    dma = pltpu.SemaphoreType.DMA
    prefill_out, decode_out = pl.pallas_call(
        functools.partial(kernel, scale, span),
        out_shape=(
            jax.ShapeDtypeStruct((2, 16, 16, 128), F32),
            jax.ShapeDtypeStruct((8, 4, 16, 128), F32),
        ),
        in_specs=[pl.BlockSpec(memory_space=pltpu.SMEM)] * 2 + [hbm] * 4,
        out_specs=(hbm, hbm),
        scratch_shapes=[
            pltpu.VMEM((2, 2, 512, 128), F32),
            pltpu.VMEM((4, 2, BLK, 128), F32),
            pltpu.VMEM((16, 2, BLK, 128), F32),
            pltpu.VMEM((128, 128), F32),
            pltpu.VMEM((8, 2, 8, 128), F32),
            pltpu.VMEM((8, 1, 128), jnp.int32),
            pltpu.VMEM((4, 2, 4, 16, 128), F32),
            pltpu.VMEM((4, 2, 2, 8, 128), F32),
            pltpu.VMEM((4, 2, 1, 128), jnp.int32),
            pltpu.VMEM((128, 8, 128), F32),
            pltpu.VMEM((16, 1, 128), jnp.int32),
            pltpu.VMEM((16, 8, 128), F32),
            pltpu.VMEM((2, HALF, 768), BF16),
            pltpu.VMEM((8, 2, BLK, 768), BF16),
            pltpu.VMEM((8, 2, 256, BLK), BF16),
            pltpu.VMEM((2, 1, HALF), jnp.int32),
            pltpu.VMEM((2, 1, HALF), F32),
            pltpu.VMEM((2, 1, HALF), F32),
            pltpu.VMEM((2, 128, HALF), F32),
            pltpu.VMEM((128, 8, 128), F32),
            dma((2,)),
            pltpu.SemaphoreType.REGULAR((3,)),
            dma((3,)),
            dma((3,)),
            dma((1,)),
            dma((1,)),
            dma((3,)),
            dma((3,)),
            dma((4,)),
            dma((4,)),
            dma((8,)),
            dma((16, PIECES)),
            dma((1,)),
            dma((1,)),
            dma((5,)),
            dma((1,)),
        ],
        compiler_params=pltpu.CompilerParams(
            collective_id=0, has_side_effects=True, vmem_limit_bytes=56 * 1024 * 1024
        ),
    )(
        lengths,
        row_length.reshape(8),
        kv_cache.reshape(2, 2, 512, 128),
        prefill_q,
        decode_q.reshape(8, 4, 16, 128),
        decode_kv.reshape(128, 128),
    )
    shapes = [prefill_out.shape, decode_out.shape]
    prefill_out, decode_out = pl.pallas_call(
        hand_over,
        out_shape=[jax.ShapeDtypeStruct(shape, F32) for shape in shapes],
        in_specs=[hbm] * 2,
        out_specs=[hbm] * 2,
        scratch_shapes=[pltpu.VMEM(shape, F32) for shape in shapes] + [dma((2,)), dma((2,))],
    )(prefill_out, decode_out)
    return prefill_out, decode_out.reshape(decode_q.shape)


def solution(mesh):
    in_specs = (
        P("head", None, "ctx", "rep", None),
        P("head", "ctx", "rep", None),
        P(None, ("ctx", "rep"), None, "head", None),
        P(None, ("ctx", "rep"), None, None, "head", None),
        P(),
        P(None, ("ctx", "rep")),
    )
    out_specs = (P("head", "ctx", "rep", None), P(None, ("ctx", "rep"), None, "head", None))
    return jax.shard_map(
        on_device, mesh=mesh, in_specs=in_specs, out_specs=out_specs, check_vma=False
    )
```
